256 devices in a mesh: frames: 16 (over z, core), mp: 16 (over y, x).
Axes of the slice: x: 4, y: 4, z: 8, core: 2. Of those that a mesh axis runs over, the one named last changes fastest.
Arguments:
- motion: bfloat16 [256, 25, 1024], P('frames', None, 'mp'), may hold values from -6 to 6
- adjacency: float32 [2, 25, 25], replicated, may hold values from -1.25 to 1.25
- w_bc: bfloat16 [2, 1024, 128], P(None, 'mp'), may hold values from -0.1875 to 0.1875
- decay: float32 [2, 256, 1024], P(None, 'frames', 'mp'), may hold values from 0.5 to 1, as said below
- skip: float32 [2, 1024], P(None, 'mp'), may hold values from 0.5 to 1.5
- w_out: bfloat16 [2, 1024, 1024], P(None, 'mp'), may hold values from -0.25 to 0.25
Outputs:
- encoded: float32 [256, 25, 1024], P('frames', None, 'mp')
The draws below stay inside these ranges and needn't reach their ends.
Inputs may be any that keep to these rules, and one draw needn't show every extreme that they name: `decay`: each entry lies strictly between 0 and 1.
All inputs are finite; a program needn't handle non-finite values.
Results may differ from the reference program's by a relative error of at most 0.012.
Values may be sent and summed in bfloat16 or wider, within the bound.
A program may use at most 64 MiB of HBM per device.

```python
import jax
import jax.numpy as jnp
from jax import lax

D = 1024
N = 64
J = 25
ENCODER_LAYERS = 2
WINDOW_LENGTH = 256


def draw_decay(key, part):
    random_keys = jax.random.split(key, 6)
    slow_share = 0.5
    slow = jax.random.uniform(random_keys[0], (ENCODER_LAYERS, 1, D)) < slow_share
    slow_rate = jnp.exp(jax.random.uniform(random_keys[1], (ENCODER_LAYERS, 1, D), jnp.float32, jnp.log(0.2 / WINDOW_LENGTH), jnp.log(1.0 / WINDOW_LENGTH)))
    fast_rate = jnp.exp(jax.random.uniform(random_keys[2], (ENCODER_LAYERS, 1, D), jnp.float32, jnp.log(1.0 / 50.0), jnp.log(1.0 / 30.0)))
    decay_speed = jnp.where(slow, slow_rate, fast_rate)
    random_noise = jax.random.uniform(random_keys[3], (ENCODER_LAYERS, WINDOW_LENGTH, D), jnp.float32, 0.5, 1.5)
    spike_position = jax.random.uniform(random_keys[4], (ENCODER_LAYERS, WINDOW_LENGTH, 1)) < 3.0 / WINDOW_LENGTH
    spike_magnitude = jax.random.uniform(random_keys[5], (ENCODER_LAYERS, WINDOW_LENGTH, 1), jnp.float32, 0.6, 0.8)
    spike_event = jnp.where(spike_position, spike_magnitude, 1.0)
    return (jnp.exp(-decay_speed * random_noise) * spike_event).astype(jnp.float32)


def with_spikes(values, key, source, target, blocks, factor):
    owner, partner = [(jnp.arange(values.shape[position]) // (values.shape[position] // blocks)).reshape([-1 if axis == position else 1 for axis in range(values.ndim)]) for position in (source, target)]
    chosen = jax.random.permutation(key, blocks)[partner]
    strong = (owner == chosen) | (owner == (partner + blocks // 2) % blocks)
    return jnp.where(strong, factor * values, values)


def shard_levels(rng, dims, pieces, least, largest):
    def one(position, blocks):
        draws = jax.random.uniform(jax.random.fold_in(jax.random.fold_in(rng, 6), position), (blocks,), jnp.float32, least / len(pieces), largest / len(pieces))
        return jnp.repeat(jnp.exp(draws), dims[position] // blocks).reshape((-1,) + (1,) * (len(dims) - position - 1))

    level = one(*pieces[0])
    for cut in pieces[1:]:
        level = level * one(*cut)
    return level


def bell_draw(key, dims, scale, bound, pieces=(), dtype=jnp.bfloat16):
    values = jax.random.normal(key, dims, jnp.float32) * scale
    if len(pieces) > 0:
        values = shard_levels(key, dims, pieces, -0.22, 0.18) * values
    return jnp.clip(values, min=-bound, max=bound).astype(dtype)


def gaussian_with(stream_key, dims, width, reach, cuts, heavy, dtype=jnp.bfloat16):
    entries = width * jax.random.normal(stream_key, dims, jnp.float32)
    if cuts:
        entries = entries * shard_levels(stream_key, dims, cuts, -0.22, 0.18)
    return jnp.clip(with_spikes(entries, jax.random.fold_in(stream_key, 3), *heavy), -reach, reach).astype(dtype)


def setup_inputs(seed: int = 0) -> dict:
    keys = jax.random.split(jax.random.key(seed), 7)
    return {
        "motion": bell_draw(keys[0], (WINDOW_LENGTH, J, D), 1.0, 6.0, ((0, 16), (2, 16))),
        "adjacency": bell_draw(keys[1], (ENCODER_LAYERS, J, J), J ** -0.5, 1.25, (), jnp.float32),
        "w_bc": bell_draw(keys[2], (ENCODER_LAYERS, D, 2 * N), D ** -0.5, 0.1875, ((1, 16),)),
        "decay": draw_decay(jax.random.fold_in(keys[6], 71), 0),
        "skip": jnp.clip(0.5 + 1.0 * jax.random.uniform(keys[4], (ENCODER_LAYERS, D), jnp.float32) ** shard_levels(keys[4], (ENCODER_LAYERS, D), ((1, 16),), -0.2, 0.2), 0.5, 1.5),
        "w_out": gaussian_with(keys[5], (ENCODER_LAYERS, D, D), D ** -0.5, 0.25, ((1, 16),), (1, 2, 16, 2.0)),
    }


def reference(motion, adjacency, w_bc, decay, skip, w_out):
    highest = lax.Precision.HIGHEST
    x = motion.astype(jnp.float32)
    for layer in range(ENCODER_LAYERS):
        mixed = jnp.einsum("jk,fkd->fjd", adjacency[layer], x, precision=highest).astype(jnp.bfloat16)
        coef = jnp.dot(mixed.reshape(-1, D), w_bc[layer], preferred_element_type=jnp.float32).reshape(WINDOW_LENGTH, J, 2 * N)
        in_b = coef[:, :, :N]
        out_c = coef[:, :, N:]
        decay_speed = decay[layer]
        drive = (1.0 - decay_speed)[:, None, :] * mixed.astype(jnp.float32)

        def advance(carry, inputs):
            a_now, d_now, b_now, c_now = inputs
            carry = a_now[None, :, None] * carry + d_now[:, :, None] * b_now[:, None, :]
            return carry, jnp.einsum("jn,jdn->jd", c_now, carry, precision=highest)

        start = jnp.zeros((J, D, N), jnp.float32)
        _, scanned = lax.scan(advance, start, (decay_speed, drive, in_b, out_c))
        result = (scanned + skip[layer][None, None, :] * mixed.astype(jnp.float32)).astype(jnp.bfloat16)
        update = jnp.dot(result.reshape(-1, D), w_out[layer], preferred_element_type=jnp.float32).reshape(WINDOW_LENGTH, J, D)
        x = x + update
    return x
```

```python
import functools

import jax
import jax.numpy as jnp
from jax import lax
from jax.experimental import pallas as pl
from jax.experimental.pallas import tpu as pltpu
from jax.sharding import PartitionSpec as P

MESH = pl.DeviceIdType.MESH
HI = lax.Precision.HIGHEST
F32, BF16 = jnp.float32, jnp.bfloat16
LAYERS = 2
G = 16
HALF, PAIR = 64, 128
FRAMES = 256
CHUNK = 128


def left_half(shape):
    return lax.broadcasted_iota(jnp.int32, shape, len(shape) - 1) % PAIR < HALF


def mix_halves(first, second):
    left = left_half(first.shape)
    return (
        jnp.where(left, first, pltpu.roll(second, HALF, 1)),
        jnp.where(left, pltpu.roll(first, HALF, 1), second),
    )


def body(
    x_ref, a_ref, wbc_ref, dec_ref, skip_ref, wout_ref, out_ref,
    xbuf, wbc, wout, dsend, dall, scale_e, scale_w, scale_x, scale_f,
    send_a, buf_a, send_b, buf_b, send_c, buf_c, send_d, buf_d, send_e, buf_e,
    tmp, xs, res, ssem, rsem,
):
    b, c = lax.axis_index("frames"), lax.axis_index("mp")

    def at(axis, peer):
        return (b, peer) if axis == "mp" else (peer, c)

    def peers(axis, act):
        me = c if axis == "mp" else b

        def one(k, carry):
            act(lax.rem(me + k, G))
            return carry

        lax.fori_loop(1, G, one, 0)

    def send(axis, n, src, dst):
        me = c if axis == "mp" else b
        peers(
            axis,
            lambda peer: pltpu.make_async_remote_copy(
                src_ref=src(peer),
                dst_ref=dst.at[me],
                send_sem=ssem.at[n],
                recv_sem=rsem.at[n],
                device_id=at(axis, peer),
                device_id_type=MESH,
            ).start(),
        )

    def wait(sem, n, dst):
        all_but_mine = dst.at[pl.ds(0, G - 1)]
        pltpu.make_async_copy(all_but_mine, all_but_mine, sem.at[n]).wait()

    barrier = pltpu.get_barrier_semaphore()
    for axis in ("mp", "frames"):
        peers(
            axis,
            lambda peer, axis=axis: pl.semaphore_signal(
                barrier, inc=1, device_id=at(axis, peer), device_id_type=MESH
            ),
        )
    dsend[...] = jnp.concatenate([dec_ref[0], dec_ref[1]], axis=1)
    pl.semaphore_wait(barrier, 2 * (G - 1))

    NX, ND, NBC, NOUT, NE, NL = 0, 1, 2, 4, 6, 7
    send("mp", NX, lambda peer: x_ref.at[peer], xbuf)
    send("mp", NBC, lambda peer: wbc_ref.at[0], wbc.at[0])
    send("frames", ND, lambda peer: dsend, dall)
    send("mp", NBC + 1, lambda peer: wbc_ref.at[1], wbc.at[1])
    for layer in range(LAYERS):
        send("mp", NOUT + layer, lambda peer, layer=layer: wout_ref.at[layer], wout.at[layer])

    xbuf[c] = x_ref[c]
    dall[b] = dsend[...]
    for layer in range(LAYERS):
        wbc[layer, c] = wbc_ref[layer]
        wout[layer, c] = wout_ref[layer]

    def spread(buf, dst, add):
        for q in range(G // 2):
            even, odd = mix_halves(buf[2 * q].astype(F32), buf[2 * q + 1].astype(F32))
            lanes = pl.ds(q * PAIR, PAIR)
            dst[pl.ds(0, G), lanes] = even.astype(dst.dtype)
            dst[pl.ds(G, G), lanes] = odd.astype(dst.dtype)

    wait(rsem, NX, xbuf)
    spread(xbuf, xs, False)

    for layer in range(LAYERS):
        base = NL + 4 * layer
        mixed = jnp.dot(a_ref[layer], xs[...], precision=HI, preferred_element_type=F32).astype(BF16)
        if layer == 0:
            wait(rsem, NBC, wbc.at[0])
        else:
            wait(rsem, NBC + 1, wbc.at[1])
        coef = jnp.dot(
            mixed, wbc[layer].reshape(G * HALF, PAIR), preferred_element_type=F32
        )
        in_b, out_c = mix_halves(coef[:G], coef[G:])
        mixed32 = mixed.astype(F32)
        for q in range(G // 2):
            lanes = slice(q * PAIR, (q + 1) * PAIR)
            pieces = mix_halves(mixed32[:G, lanes], mixed32[G:, lanes])
            for i in range(2):
                send_a[layer, 2 * q + i, :, pl.ds(0, PAIR)] = pieces[i].astype(BF16)
                send_a[layer, 2 * q + i, :, pl.ds(PAIR, PAIR)] = in_b.astype(BF16)
                send_a[layer, 2 * q + i, :, pl.ds(2 * PAIR, PAIR)] = out_c.astype(BF16)
        send("mp", base, lambda peer: send_a.at[layer, peer], buf_a.at[layer])
        buf_a[layer, c] = send_a[layer, c]

        if layer == 0:
            wait(rsem, ND, dall)
            a = dall[...].reshape(FRAMES, PAIR)
            later = lax.broadcasted_iota(jnp.int32, (FRAMES, FRAMES), 0)
            earlier = lax.broadcasted_iota(jnp.int32, (FRAMES, FRAMES), 1)
            logs = jnp.dot(
                (earlier <= later).astype(F32), jnp.log(a), precision=HI, preferred_element_type=F32
            )
            for l in range(LAYERS):
                lanes = left_half((FRAMES, PAIR))
                mine = lanes if l == 0 else jnp.logical_not(lanes)
                la = jnp.where(mine, logs, pltpu.roll(logs, HALF, 1))
                da = 1.0 - jnp.where(mine, a, pltpu.roll(a, HALF, 1))
                for t in range(FRAMES // CHUNK):
                    rows = slice(t * CHUNK, (t + 1) * CHUNK)
                    rel = la[rows] - la[t * CHUNK + CHUNK // 2 - 1 : t * CHUNK + CHUNK // 2]
                    scale_e[l, pl.ds(t * CHUNK, CHUNK)] = jnp.exp(rel)
                    scale_w[l, pl.ds(t * CHUNK, CHUNK)] = da[rows] * jnp.exp(-rel)
                end = la[CHUNK - 1 : CHUNK]
                scale_x[l] = da[:CHUNK] * jnp.exp(end - la[:CHUNK])
                scale_f[l] = jnp.exp(la[CHUNK:] - end)

        wait(rsem, base, buf_a.at[layer])
        for part in range(3):
            tmp[part] = buf_a[layer, :, :, pl.ds(part * PAIR, PAIR)].reshape(FRAMES, PAIR).astype(F32)
        for pair in range(G):
            for part in range(3):
                send_b[layer, pair, :, pl.ds(part * PAIR, PAIR)] = tmp[
                    part, pl.ds(pair, G, stride=G), :
                ].astype(BF16)
        send("frames", base + 1, lambda peer: send_b.at[layer, peer], buf_b.at[layer])
        buf_b[layer, b] = send_b[layer, b]

        wait(rsem, base + 1, buf_b.at[layer])
        rows = buf_b[layer].reshape(FRAMES, 3 * PAIR)
        m, bp, cp = rows[:, :PAIR].astype(F32), rows[:, PAIR : 2 * PAIR], rows[:, 2 * PAIR :]
        v = (m * scale_w[layer]).astype(BF16)
        vx = (m[:CHUNK] * scale_x[layer]).astype(BF16)
        left = left_half((FRAMES, PAIR))
        c32 = cp.astype(F32)
        causal = lax.broadcasted_iota(jnp.int32, (CHUNK, CHUNK), 1) <= lax.broadcasted_iota(
            jnp.int32, (CHUNK, CHUNK), 0
        )
        over_n = (((1,), (1,)), ((), ()))

        def product(cj, bj, value, masked):
            grid = lax.dot_general(cj, bj, over_n, preferred_element_type=F32)
            if masked:
                grid = jnp.where(causal, grid, 0.0)
            return jnp.dot(grid.astype(BF16), value, preferred_element_type=F32)

        both = []
        for j in range(2):
            cj = jnp.where(left if j == 0 else jnp.logical_not(left), c32, 0.0).astype(BF16)
            y0 = product(cj[:CHUNK], bp[:CHUNK], v[:CHUNK], True)
            y1 = product(cj[CHUNK:], bp[CHUNK:], v[CHUNK:], True)
            yx = product(cj[CHUNK:], bp[:CHUNK], vx, False)
            both.append((y0, y1, yx))
        half = left[:CHUNK]
        y0, y1, yx = [jnp.where(half, p, q) for p, q in zip(*both)]
        gain = skip_ref[pl.ds(layer, 1), :]
        gain = jnp.concatenate([gain, gain], axis=1)
        low = y0 * scale_e[layer, pl.ds(0, CHUNK)] + gain * m[:CHUNK]
        high = (
            y1 * scale_e[layer, pl.ds(CHUNK, CHUNK)] + yx * scale_f[layer] + gain * m[CHUNK:]
        )
        send_c[layer, pl.ds(0, G // 2)] = low.astype(BF16).reshape(G // 2, G, PAIR)
        send_c[layer, pl.ds(G // 2, G // 2)] = high.astype(BF16).reshape(G // 2, G, PAIR)
        send("frames", base + 2, lambda peer: send_c.at[layer, peer], buf_c.at[layer])
        buf_c[layer, b] = send_c[layer, b]

        wait(rsem, base + 2, buf_c.at[layer])
        tmp[0] = buf_c[layer].reshape(FRAMES, PAIR).astype(F32)
        for frame in range(G):
            send_d[layer, frame] = tmp[0, pl.ds(frame, G, stride=G), :].astype(BF16)
        send("mp", base + 3, lambda peer: send_d.at[layer, peer], buf_d.at[layer])
        buf_d[layer, c] = send_d[layer, c]

        wait(rsem, NOUT + layer, wout.at[layer])
        wait(rsem, base + 3, buf_d.at[layer])
        spread(buf_d.at[layer], res, False)
        xs[...] += jnp.dot(
            res[...], wout[layer].reshape(G * HALF, G * HALF), preferred_element_type=F32
        )

    for q in range(G // 2):
        lanes = pl.ds(q * PAIR, PAIR)
        pieces = mix_halves(xs[pl.ds(0, G), lanes], xs[pl.ds(G, G), lanes])
        send_e[2 * q] = pieces[0]
        send_e[2 * q + 1] = pieces[1]
    send("mp", NE, lambda peer: send_e.at[peer], buf_e)
    buf_e[c] = send_e[c]
    wait(ssem, NX, xbuf)
    wait(ssem, ND, dall)
    for layer in range(LAYERS):
        base = NL + 4 * layer
        wait(ssem, NBC + layer, wbc.at[layer])
        wait(ssem, NOUT + layer, wout.at[layer])
        wait(ssem, base, buf_a.at[layer])
        wait(ssem, base + 1, buf_b.at[layer])
        wait(ssem, base + 2, buf_c.at[layer])
        wait(ssem, base + 3, buf_d.at[layer])
    wait(ssem, NE, buf_e)
    wait(rsem, NE, buf_e)
    out_ref[...] = buf_e[...]


def shards(motion, adjacency, w_bc, decay, skip, w_out):
    frames, joints, width = motion.shape
    more = 2 * G - joints
    x = jnp.pad(motion, ((0, 0), (0, more), (0, 0))).reshape(frames, G, PAIR)
    a = jnp.pad(adjacency, ((0, 0), (0, more), (0, more)))
    a = a.reshape(LAYERS, G, 2, G, 2).transpose(0, 2, 1, 4, 3).reshape(LAYERS, 2 * G, 2 * G)
    vm = pltpu.VMEM
    out = pl.pallas_call(
        body,
        out_shape=jax.ShapeDtypeStruct((G, G, PAIR), F32),
        in_specs=[pl.BlockSpec(memory_space=vm)] * 6,
        out_specs=pl.BlockSpec(memory_space=vm),
        scratch_shapes=[
            vm((G, G, PAIR), BF16),
            vm((LAYERS, G, HALF, PAIR), BF16),
            vm((LAYERS, G, HALF, G * HALF), BF16),
            vm((G, PAIR), F32),
            vm((G, G, PAIR), F32),
            vm((LAYERS, FRAMES, PAIR), F32),
            vm((LAYERS, FRAMES, PAIR), F32),
            vm((LAYERS, CHUNK, PAIR), F32),
            vm((LAYERS, CHUNK, PAIR), F32),
            vm((LAYERS, G, G, 3 * PAIR), BF16),
            vm((LAYERS, G, G, 3 * PAIR), BF16),
            vm((LAYERS, G, G, 3 * PAIR), BF16),
            vm((LAYERS, G, G, 3 * PAIR), BF16),
            vm((LAYERS, G, G, PAIR), BF16),
            vm((LAYERS, G, G, PAIR), BF16),
            vm((LAYERS, G, G, PAIR), BF16),
            vm((LAYERS, G, G, PAIR), BF16),
            vm((G, G, PAIR), F32),
            vm((G, G, PAIR), F32),
            vm((3, FRAMES, PAIR), F32),
            vm((2 * G, G * HALF), F32),
            vm((2 * G, G * HALF), BF16),
            pltpu.SemaphoreType.DMA((15,)),
            pltpu.SemaphoreType.DMA((15,)),
        ],
        compiler_params=pltpu.CompilerParams(
            collective_id=0, has_side_effects=True, vmem_limit_bytes=40 * 2**20
        ),
    )(x, a, w_bc, decay, skip, w_out)
    return out.reshape(frames, 2 * G, width)[:, :joints]


def solution(mesh):
    return jax.shard_map(
        shards,
        mesh=mesh,
        in_specs=(
            P("frames", None, "mp"),
            P(),
            P(None, "mp", None),
            P(None, "frames", "mp"),
            P(None, "mp"),
            P(None, "mp", None),
        ),
        out_specs=P("frames", None, "mp"),
        check_vma=False,
    )
```

```python
import jax
import jax.numpy as jnp
from jax import lax
from jax.experimental import pallas as pl
from jax.experimental.pallas import tpu as pltpu
from jax.sharding import PartitionSpec as P

MESH = pl.DeviceIdType.MESH
HI = lax.Precision.HIGHEST
F32, BF16 = jnp.float32, jnp.bfloat16
LAYERS = 2
JOINTS = 25
G = 16
SIDE = 4
USED = 13
HALF, PAIR = 64, 128
WIDE = G * HALF
FRAMES = 256
CHUNK = 128


def left_half(shape):
    return lax.broadcasted_iota(jnp.int32, shape, len(shape) - 1) % PAIR < HALF


def mix_halves(first, second):
    left = left_half(first.shape)
    return (
        jnp.where(left, first, pltpu.roll(second, HALF, 1)),
        jnp.where(left, pltpu.roll(first, HALF, 1), second),
    )


def body(
    x_hbm, a_hbm, wbc_hbm, dec_hbm, skip_hbm, wout_hbm, out_ref,
    xin, ain, din, skip, wb0, blk0, blk1, dsend, dall,
    scale_e, scale_w, scale_x, scale_f, aperm,
    send_x, buf_x, send_a, buf_a, send_k, buf_k, send_g, buf_g,
    send_b, buf_b, send_c, buf_c, send_d, buf_d, send_e, buf_e,
    tmp, xs, res, lsem, ssem, rsem,
):
    b, c = lax.axis_index("frames"), lax.axis_index("mp")
    core = lax.rem(b, 2)
    cy, cx = c // SIDE, lax.rem(c, SIDE)
    scans = b < USED

    loads = {}

    def load(name, src, dst):
        loads[name] = pltpu.make_async_copy(src, dst, lsem.at[len(loads)])
        loads[name].start()

    load("x", x_hbm, xin)
    load("wb0", wbc_hbm.at[0], wb0.at[cy, cx])
    load("dec", dec_hbm, din)
    load("a", a_hbm, ain)
    load("skip", skip_hbm, skip)
    load("out0", wout_hbm.at[0], blk0.at[cy, cx, :, :, pl.ds(0, WIDE)])
    load("bc1", wbc_hbm.at[1], blk0.at[cy, cx, :, :, pl.ds(WIDE, PAIR)])
    load("out1", wout_hbm.at[1], blk1.at[cy, cx])

    def at(axis, peer):
        return (b, peer) if axis == "mp" else (peer, c)

    def peers(axis, act):
        me = c if axis == "mp" else b

        def one(k, carry):
            act(lax.rem(me + k, G))
            return carry

        lax.fori_loop(1, G, one, 0)

    names = []

    def number(name):
        if name not in names:
            names.append(name)
        return names.index(name)

    def copy(name, src, dst, device):
        return pltpu.make_async_remote_copy(
            src_ref=src,
            dst_ref=dst,
            send_sem=ssem.at[number(name)],
            recv_sem=rsem.at[number(name)],
            device_id=device,
            device_id_type=MESH,
        )

    def wait_bytes(sem, name, ref):
        pltpu.make_async_copy(ref, ref, sem.at[number(name)]).wait()

    drains = []

    def send(axis, name, src, dst):
        me = c if axis == "mp" else b
        peers(axis, lambda peer: copy(name, src(peer), dst.at[me], at(axis, peer)).start())
        drains.append(lambda: wait_bytes(ssem, name, dst.at[pl.ds(0, G - 1)]))

    def send_used(name, src, dst):
        def act(peer):
            @pl.when(peer < USED)
            def _():
                copy(name, src(peer), dst.at[b], (peer, c)).start()

        peers("frames", act)

        def drain():
            @pl.when(scans)
            def _():
                wait_bytes(ssem, name, dst.at[pl.ds(0, USED - 1)])

            @pl.when(jnp.logical_not(scans))
            def _():
                wait_bytes(ssem, name, dst.at[pl.ds(0, USED)])

        drains.append(drain)

    def arrived(name, dst):
        wait_bytes(rsem, name, dst.at[pl.ds(0, G - 1)])

    barrier = pltpu.get_barrier_semaphore()
    for axis in ("frames", "mp"):
        peers(
            axis,
            lambda peer, axis=axis: pl.semaphore_signal(
                barrier, inc=1, device_id=at(axis, peer), device_id_type=MESH
            ),
        )

    loads["x"].wait()
    for pair in range(G):
        if pair < USED:
            even = xin[2 * pair].astype(F32)
            odd = xin[2 * pair + 1].astype(F32) if 2 * pair + 1 < JOINTS else jnp.zeros_like(even)
            tmp[0, pl.ds(pair * G, G)] = jnp.concatenate([even, odd], axis=1)
        else:
            tmp[0, pl.ds(pair * G, G)] = jnp.zeros((G, PAIR), F32)
    for frame in range(G):
        send_x[frame] = tmp[0, pl.ds(frame, G, stride=G), :].astype(BF16)
    loads["dec"].wait()
    dsend[...] = jnp.concatenate([din[0], din[1]], axis=1)
    loads["a"].wait()
    row = lax.broadcasted_iota(jnp.int32, (2 * G, JOINTS), 0)
    pick = (lax.broadcasted_iota(jnp.int32, (2 * G, JOINTS), 1) == 2 * lax.rem(row, G) + row // G).astype(F32)
    for layer in range(LAYERS):
        half = jnp.dot(pick, ain[layer], precision=HI, preferred_element_type=F32)
        aperm[layer] = lax.dot_general(
            half, pick, (((1,), (1,)), ((), ())), precision=HI, preferred_element_type=F32
        )
    for name in ("wb0", "skip", "out0", "bc1", "out1"):
        loads[name].wait()
    for layer in range(LAYERS):
        buf_c[layer, pl.ds(USED, G - USED)] = jnp.zeros((G - USED, G, PAIR), BF16)
    buf_x[c] = send_x[c]
    dall[b] = dsend[...]

    pl.semaphore_wait(barrier, 2 * (G - 1))

    send("mp", "x", lambda peer: send_x.at[peer], buf_x)
    peers("mp", lambda peer: copy("wb0", wb0.at[cy, cx], wb0.at[cy, cx], at("mp", peer)).start())

    def wait_wb0(sem):
        wait_bytes(sem, "wb0", flat_wb0)

    flat_wb0 = wb0.reshape(G, 2, HALF // 2, PAIR).at[pl.ds(0, G - 1)]
    drains.append(lambda: wait_wb0(ssem))
    send("frames", "dec", lambda peer: dsend, dall)

    blocks = (blk0, blk1)

    def step1(n):
        blk = blocks[n]
        for i in range(1, SIDE):
            to = lax.rem(cy + i * core, SIDE) * SIDE + lax.rem(cx + i * (1 - core), SIDE)
            part = blk.at[cy, cx, core]
            copy(f"one{n}", part, part, (b, to)).start()
        drains.append(lambda: wait_bytes(ssem, f"one{n}", blk.at[0, pl.ds(0, SIDE - 1), 0]))

    def step2(n):
        blk = blocks[n]
        wait_bytes(rsem, f"one{n}", blk.at[0, pl.ds(0, SIDE - 1), 0])

        @pl.when(core == 0)
        def _():
            for i in range(1, SIDE):
                part = blk.at[cy, :, 0]
                copy(f"two{n}", part, part, (b, lax.rem(cy + i, SIDE) * SIDE + cx)).start()

        @pl.when(core == 1)
        def _():
            for i in range(1, SIDE):
                part = blk.at[:, cx, 1]
                copy(f"two{n}", part, part, (b, cy * SIDE + lax.rem(cx + i, SIDE))).start()

        drains.append(lambda: wait_bytes(ssem, f"two{n}", blk.at[pl.ds(0, SIDE - 1), :, 0]))

    def step3(n):
        blk = blocks[n]
        wait_bytes(rsem, f"two{n}", blk.at[pl.ds(0, SIDE - 1), :, 0])
        part = blk.at[:, :, core]
        copy(f"three{n}", part, part, (b + 1 - 2 * core, c)).start()
        drains.append(lambda: wait_bytes(ssem, f"three{n}", blk.at[:, :, 0]))

    def step4(n):
        wait_bytes(rsem, f"three{n}", blocks[n].at[:, :, 0])

    for n in range(2):
        step1(n)

    def spread(buf, dst):
        for q in range(G // 2):
            even, odd = mix_halves(buf[2 * q].astype(F32), buf[2 * q + 1].astype(F32))
            lanes = pl.ds(q * PAIR, PAIR)
            dst[pl.ds(0, G), lanes] = even.astype(dst.dtype)
            dst[pl.ds(G, G), lanes] = odd.astype(dst.dtype)

    def decay_scales():
        arrived("dec", dall)
        a = dall[...].reshape(FRAMES, PAIR)
        later = lax.broadcasted_iota(jnp.int32, (FRAMES, FRAMES), 0)
        earlier = lax.broadcasted_iota(jnp.int32, (FRAMES, FRAMES), 1)
        logs = jnp.dot(
            (earlier <= later).astype(F32), jnp.log(a), precision=HI, preferred_element_type=F32
        )
        for l in range(LAYERS):
            left = left_half((FRAMES, PAIR))
            mine = left if l == 0 else jnp.logical_not(left)
            la = jnp.where(mine, logs, pltpu.roll(logs, HALF, 1))
            da = 1.0 - jnp.where(mine, a, pltpu.roll(a, HALF, 1))
            for t in range(FRAMES // CHUNK):
                rows = slice(t * CHUNK, (t + 1) * CHUNK)
                rel = la[rows] - la[t * CHUNK + CHUNK // 2 - 1 : t * CHUNK + CHUNK // 2]
                scale_e[l, pl.ds(t * CHUNK, CHUNK)] = jnp.exp(rel)
                scale_w[l, pl.ds(t * CHUNK, CHUNK)] = da[rows] * jnp.exp(-rel)
            end = la[CHUNK - 1 : CHUNK]
            scale_x[l] = da[:CHUNK] * jnp.exp(end - la[:CHUNK])
            scale_f[l] = jnp.exp(la[CHUNK:] - end)

    arrived("x", buf_x)
    spread(buf_x, xs)

    for layer in range(LAYERS):

        def named(name, layer=layer):
            return f"{name}{layer}"

        mixed32 = jnp.dot(aperm[layer], xs[...], precision=HI, preferred_element_type=F32)
        mixed = mixed32.astype(BF16)
        mixed32 = mixed.astype(F32)
        for q in range(G // 2):
            lanes = slice(q * PAIR, (q + 1) * PAIR)
            pieces = mix_halves(mixed32[:G, lanes], mixed32[G:, lanes])
            for i in range(2):
                send_a[layer, 2 * q + i] = pieces[i].astype(BF16)
        send("mp", named("a"), lambda peer: send_a.at[layer, peer], buf_a.at[layer])
        buf_a[layer, c] = send_a[layer, c]
        if layer == 0:
            wait_wb0(rsem)
            weights = wb0[...].reshape(WIDE, PAIR)
        else:
            weights = blk0[:, :, :, :, pl.ds(WIDE, PAIR)].reshape(WIDE, PAIR)
        coef = jnp.dot(mixed, weights, preferred_element_type=F32)
        in_b, out_c = mix_halves(coef[:G], coef[G:])
        for pair in range(USED):
            send_k[layer, pair, :, pl.ds(0, PAIR)] = in_b[pair : pair + 1]
            send_k[layer, pair, :, pl.ds(PAIR, PAIR)] = out_c[pair : pair + 1]
        send_used(named("k"), lambda peer: send_k.at[layer, peer], buf_k.at[layer])

        arrived(named("a"), buf_a.at[layer])
        tmp[0] = buf_a[layer].reshape(FRAMES, PAIR).astype(F32)
        for pair in range(USED):
            send_b[layer, pair] = tmp[0, pl.ds(pair, G, stride=G), :].astype(BF16)
        send_used(named("b"), lambda peer: send_b.at[layer, peer], buf_b.at[layer])

        @pl.when(scans)
        def _():
            buf_b[layer, b] = send_b[layer, b]
            buf_k[layer, b] = send_k[layer, b]
            arrived(named("k"), buf_k.at[layer])
            for block in range(G):
                for part in range(2):
                    tmp[1 + part, pl.ds(block, 1)] = buf_k[layer, block, :, pl.ds(part * PAIR, PAIR)]
            for part in range(2):
                send_g[layer, :, pl.ds(part * PAIR, PAIR)] = tmp[1 + part, pl.ds(0, G)].astype(BF16)
            peers(
                "mp",
                lambda peer: copy(
                    named("g"), send_g.at[layer], buf_g.at[layer, c], (b, peer)
                ).start(),
            )
            buf_g[layer, c] = send_g[layer]

        def drain_g(layer=layer):
            @pl.when(scans)
            def _():
                wait_bytes(ssem, f"g{layer}", buf_g.at[layer, pl.ds(0, G - 1)])

        drains.append(drain_g)
        step2(layer)
        if layer == 0:
            decay_scales()

        @pl.when(scans)
        def _():
            arrived(named("g"), buf_g.at[layer])
            for part in range(2):
                tmp[1 + part] = buf_g[layer, :, :, pl.ds(part * PAIR, PAIR)].reshape(FRAMES, PAIR).astype(F32)
            bp, cp = [
                jnp.concatenate([tmp[1 + part, pl.ds(k, G, stride=G), :] for k in range(G)], axis=0)
                for part in range(2)
            ]
            bp = bp.astype(BF16)
            left = left_half((FRAMES, PAIR))
            causal = lax.broadcasted_iota(jnp.int32, (CHUNK, CHUNK), 1) <= lax.broadcasted_iota(
                jnp.int32, (CHUNK, CHUNK), 0
            )

            def grid(cj, bj, masked):
                g = lax.dot_general(
                    cj, bj, (((1,), (1,)), ((), ())), preferred_element_type=F32
                )
                return (jnp.where(causal, g, 0.0) if masked else g).astype(BF16)

            grids = []
            for j in range(2):
                cj = jnp.where(left if j == 0 else jnp.logical_not(left), cp, 0.0).astype(BF16)
                grids.append(
                    (
                        grid(cj[:CHUNK], bp[:CHUNK], True),
                        grid(cj[CHUNK:], bp[CHUNK:], True),
                        grid(cj[CHUNK:], bp[:CHUNK], False),
                    )
                )
            arrived(named("b"), buf_b.at[layer])
            m = buf_b[layer].reshape(FRAMES, PAIR).astype(F32)
            v = (m * scale_w[layer]).astype(BF16)
            vx = (m[:CHUNK] * scale_x[layer]).astype(BF16)
            values = (v[:CHUNK], v[CHUNK:], vx)
            y0, y1, yx = [
                jnp.where(
                    left[:CHUNK],
                    jnp.dot(grids[0][i], values[i], preferred_element_type=F32),
                    jnp.dot(grids[1][i], values[i], preferred_element_type=F32),
                )
                for i in range(3)
            ]
            gain = skip[pl.ds(layer, 1), :]
            gain = jnp.concatenate([gain, gain], axis=1)
            low = y0 * scale_e[layer, pl.ds(0, CHUNK)] + gain * m[:CHUNK]
            high = (
                y1 * scale_e[layer, pl.ds(CHUNK, CHUNK)] + yx * scale_f[layer] + gain * m[CHUNK:]
            )
            send_c[layer, pl.ds(0, G // 2)] = low.astype(BF16).reshape(G // 2, G, PAIR)
            send_c[layer, pl.ds(G // 2, G // 2)] = high.astype(BF16).reshape(G // 2, G, PAIR)
            peers(
                "frames",
                lambda peer: copy(
                    named("c"), send_c.at[layer, peer], buf_c.at[layer, b], (peer, c)
                ).start(),
            )
            buf_c[layer, b] = send_c[layer, b]

        def drain_c(layer=layer):
            @pl.when(scans)
            def _():
                wait_bytes(ssem, f"c{layer}", buf_c.at[layer, pl.ds(0, G - 1)])

        drains.append(drain_c)
        step3(layer)

        @pl.when(scans)
        def _():
            wait_bytes(rsem, named("c"), buf_c.at[layer, pl.ds(0, USED - 1)])

        @pl.when(jnp.logical_not(scans))
        def _():
            wait_bytes(rsem, named("c"), buf_c.at[layer, pl.ds(0, USED)])

        tmp[0] = buf_c[layer].reshape(FRAMES, PAIR).astype(F32)
        for frame in range(G):
            send_d[layer, frame] = tmp[0, pl.ds(frame, G, stride=G), :].astype(BF16)
        send("mp", named("d"), lambda peer: send_d.at[layer, peer], buf_d.at[layer])
        buf_d[layer, c] = send_d[layer, c]

        step4(layer)
        arrived(named("d"), buf_d.at[layer])
        spread(buf_d.at[layer], res)
        weights = blocks[layer][:, :, :, :, pl.ds(0, WIDE)].reshape(WIDE, WIDE)
        xs[...] += jnp.dot(res[...], weights, preferred_element_type=F32)

    for q in range(G // 2):
        lanes = pl.ds(q * PAIR, PAIR)
        pieces = mix_halves(xs[pl.ds(0, G), lanes], xs[pl.ds(G, G), lanes])
        send_e[2 * q] = pieces[0]
        send_e[2 * q + 1] = pieces[1]
    send("mp", "e", lambda peer: send_e.at[peer], buf_e)
    buf_e[c] = send_e[c]
    for drain in drains:
        drain()
    arrived("e", buf_e)
    tmp[0] = buf_e[...].reshape(FRAMES, PAIR)
    for pair in range(USED):
        both = tmp[0, pl.ds(pair, G, stride=G), :]
        out_ref[2 * pair] = both[:, :HALF]
        if 2 * pair + 1 < JOINTS:
            out_ref[2 * pair + 1] = both[:, HALF:]


def shards(motion, adjacency, w_bc, decay, skip, w_out):
    vm = pltpu.VMEM
    part = HALF // 2
    out = pl.pallas_call(
        body,
        out_shape=jax.ShapeDtypeStruct((JOINTS, G, HALF), F32),
        in_specs=[pl.BlockSpec(memory_space=pltpu.HBM)] * 6,
        out_specs=pl.BlockSpec(memory_space=vm),
        scratch_shapes=[
            vm((JOINTS, G, HALF), BF16),
            vm((LAYERS, JOINTS, JOINTS), F32),
            vm((LAYERS, G, HALF), F32),
            vm((LAYERS, HALF), F32),
            vm((SIDE, SIDE, 2, part, PAIR), BF16),
            vm((SIDE, SIDE, 2, part, WIDE + PAIR), BF16),
            vm((SIDE, SIDE, 2, part, WIDE), BF16),
            vm((G, PAIR), F32),
            vm((G, G, PAIR), F32),
            vm((LAYERS, FRAMES, PAIR), F32),
            vm((LAYERS, FRAMES, PAIR), F32),
            vm((LAYERS, CHUNK, PAIR), F32),
            vm((LAYERS, CHUNK, PAIR), F32),
            vm((LAYERS, 2 * G, 2 * G), F32),
            vm((G, G, PAIR), BF16),
            vm((G, G, PAIR), BF16),
            vm((LAYERS, G, G, PAIR), BF16),
            vm((LAYERS, G, G, PAIR), BF16),
            vm((LAYERS, USED, 1, 2 * PAIR), F32),
            vm((LAYERS, G, 1, 2 * PAIR), F32),
            vm((LAYERS, G, 2 * PAIR), BF16),
            vm((LAYERS, G, G, 2 * PAIR), BF16),
            vm((LAYERS, USED, G, PAIR), BF16),
            vm((LAYERS, G, G, PAIR), BF16),
            vm((LAYERS, G, G, PAIR), BF16),
            vm((LAYERS, G, G, PAIR), BF16),
            vm((LAYERS, G, G, PAIR), BF16),
            vm((LAYERS, G, G, PAIR), BF16),
            vm((G, G, PAIR), F32),
            vm((G, G, PAIR), F32),
            vm((3, FRAMES, PAIR), F32),
            vm((2 * G, WIDE), F32),
            vm((2 * G, WIDE), BF16),
            pltpu.SemaphoreType.DMA((8,)),
            pltpu.SemaphoreType.DMA((24,)),
            pltpu.SemaphoreType.DMA((24,)),
        ],
        compiler_params=pltpu.CompilerParams(
            collective_id=0, has_side_effects=True, vmem_limit_bytes=40 * 2**20
        ),
    )(
        motion.transpose(1, 0, 2),
        adjacency,
        w_bc.reshape(LAYERS, 2, part, PAIR),
        decay,
        skip,
        w_out.reshape(LAYERS, 2, part, WIDE),
    )
    return out.transpose(1, 0, 2)


def solution(mesh):
    return jax.shard_map(
        shards,
        mesh=mesh,
        in_specs=(
            P("frames", None, "mp"),
            P(),
            P(None, "mp", None),
            P(None, "frames", "mp"),
            P(None, "mp"),
            P(None, "mp", None),
        ),
        out_specs=P("frames", None, "mp"),
        check_vma=False,
    )
```

```python
import jax
import jax.numpy as jnp
from jax import lax
from jax.experimental import pallas as pl
from jax.experimental.pallas import tpu as pltpu
from jax.sharding import PartitionSpec as P

MESH = pl.DeviceIdType.MESH
HI = lax.Precision.HIGHEST
F32, BF16 = jnp.float32, jnp.bfloat16
LAYERS = 2
JOINTS = 25
G = 16
SIDE = 4
USED = 13
HALF, PAIR = 64, 128
WIDE = G * HALF
FRAMES = 256
CHUNK = 128


def left_half(shape):
    return lax.broadcasted_iota(jnp.int32, shape, len(shape) - 1) % PAIR < HALF


def mix_halves(first, second):
    left = left_half(first.shape)
    return (
        jnp.where(left, first, pltpu.roll(second, HALF, 1)),
        jnp.where(left, pltpu.roll(first, HALF, 1), second),
    )


def body(
    x_hbm, a_hbm, wbc_hbm, dec_hbm, skip_hbm, wout_hbm, out_ref,
    xin, araw, ain, din, skip, wb0, blk0, blk1, dsend, dall,
    scale_e, scale_w, scale_x, scale_f, aperm,
    send_x, buf_x, send_a, buf_a, send_k, buf_k, send_g, buf_g,
    send_b, buf_b, send_c, buf_c, send_d, buf_d, send_e, buf_e,
    tmp, xs, res, lsem, ssem, rsem,
):
    b, c = lax.axis_index("frames"), lax.axis_index("mp")
    core = lax.rem(b, 2)
    cy, cx = c // SIDE, lax.rem(c, SIDE)
    scans = b < USED

    loads = {}

    def load(name, src, dst):
        loads[name] = pltpu.make_async_copy(src, dst, lsem.at[len(loads)])
        loads[name].start()

    load("x", x_hbm, xin)
    load("wb0", wbc_hbm.at[0], wb0.at[cy, cx])
    load("dec", dec_hbm, din)
    load("a", a_hbm, araw)
    load("skip", skip_hbm, skip)
    load("out0", wout_hbm.at[0, core], blk0.at[cy, cx, core, :, pl.ds(0, WIDE)])
    load("bc1", wbc_hbm.at[1, core], blk0.at[cy, cx, core, :, pl.ds(WIDE, PAIR)])
    load("out1", wout_hbm.at[1, core], blk1.at[cy, cx, core])

    def at(axis, peer):
        return (b, peer) if axis == "mp" else (peer, c)

    def peers(axis, act):
        def off(k, half):
            return half + (k + 1) // 2 * (1 - 2 * lax.rem(k + 1, 2))

        def one(k, carry):
            if axis == "mp":
                to_y = lax.rem(cy + off(k // SIDE, SIDE // 2), SIDE)
                to_x = lax.rem(cx + off(lax.rem(k, SIDE), SIDE // 2), SIDE)
                act(to_y * SIDE + to_x)
            else:
                act(lax.rem(b + off(k, G // 2), G))
            return carry

        lax.fori_loop(0, G - 1, one, 0)

    names = []

    def number(name):
        if name not in names:
            names.append(name)
        return names.index(name)

    def copy(name, src, dst, device):
        return pltpu.make_async_remote_copy(
            src_ref=src,
            dst_ref=dst,
            send_sem=ssem.at[number(name)],
            recv_sem=rsem.at[number(name)],
            device_id=device,
            device_id_type=MESH,
        )

    def wait_bytes(sem, name, ref):
        pltpu.make_async_copy(ref, ref, sem.at[number(name)]).wait()

    drains = []

    def send(axis, name, src, dst):
        me = c if axis == "mp" else b
        peers(axis, lambda peer: copy(name, src(peer), dst.at[me], at(axis, peer)).start())
        drains.append(lambda: wait_bytes(ssem, name, dst.at[pl.ds(0, G - 1)]))

    def send_used(name, src, dst):
        def act(peer):
            @pl.when(peer < USED)
            def _():
                copy(name, src(peer), dst.at[b], (peer, c)).start()

        peers("frames", act)

        def drain():
            @pl.when(scans)
            def _():
                wait_bytes(ssem, name, dst.at[pl.ds(0, USED - 1)])

            @pl.when(jnp.logical_not(scans))
            def _():
                wait_bytes(ssem, name, dst.at[pl.ds(0, USED)])

        drains.append(drain)

    def arrived(name, dst):
        wait_bytes(rsem, name, dst.at[pl.ds(0, G - 1)])

    barrier = pltpu.get_barrier_semaphore()
    for axis in ("frames", "mp"):
        peers(
            axis,
            lambda peer, axis=axis: pl.semaphore_signal(
                barrier, inc=1, device_id=at(axis, peer), device_id_type=MESH
            ),
        )

    loads["x"].wait()
    for pair in range(G):
        if pair < USED:
            even = xin[2 * pair].astype(F32)
            odd = xin[2 * pair + 1].astype(F32) if 2 * pair + 1 < JOINTS else jnp.zeros_like(even)
            tmp[0, pl.ds(pair * G, G)] = jnp.concatenate([even, odd], axis=1)
        else:
            tmp[0, pl.ds(pair * G, G)] = jnp.zeros((G, PAIR), F32)
    for frame in range(G):
        send_x[frame] = tmp[0, pl.ds(frame, G, stride=G), :].astype(BF16)
    buf_x[c] = send_x[c]

    pl.semaphore_wait(barrier, 2 * (G - 1))

    send("mp", "x", lambda peer: send_x.at[peer], buf_x)
    loads["wb0"].wait()
    peers("mp", lambda peer: copy("wb0", wb0.at[cy, cx], wb0.at[cy, cx], at("mp", peer)).start())
    flat_wb0 = wb0.reshape(G, 2, HALF // 2, PAIR).at[pl.ds(0, G - 1)]
    drains.append(lambda: wait_bytes(ssem, "wb0", flat_wb0))
    loads["dec"].wait()
    dsend[...] = jnp.concatenate([din[0], din[1]], axis=1)
    send("frames", "dec", lambda peer: dsend, dall)
    dall[b] = dsend[...]
    loads["a"].wait()
    for joint in range(JOINTS):
        for layer in range(LAYERS):
            ain[layer, pl.ds(joint, 1)] = araw[joint, pl.ds(layer, 1)]
    row = lax.broadcasted_iota(jnp.int32, (2 * G, JOINTS), 0)
    pick = (lax.broadcasted_iota(jnp.int32, (2 * G, JOINTS), 1) == 2 * lax.rem(row, G) + row // G).astype(F32)
    for layer in range(LAYERS):
        half = jnp.dot(pick, ain[layer], precision=HI, preferred_element_type=F32)
        aperm[layer] = lax.dot_general(
            half, pick, (((1,), (1,)), ((), ())), precision=HI, preferred_element_type=F32
        )
        buf_c[layer, pl.ds(USED, G - USED)] = jnp.zeros((G - USED, G, PAIR), BF16)
    for name in ("skip", "out0", "bc1", "out1"):
        loads[name].wait()

    blocks = (blk0, blk1)

    def step1(n):
        blk = blocks[n]
        for i in range(1, SIDE):
            to = lax.rem(cy + i * core, SIDE) * SIDE + lax.rem(cx + i * (1 - core), SIDE)
            part = blk.at[cy, cx, core]
            copy(f"one{n}", part, part, (b, to)).start()
        drains.append(lambda: wait_bytes(ssem, f"one{n}", blk.at[0, pl.ds(0, SIDE - 1), 0]))

    def step2(n):
        blk = blocks[n]
        wait_bytes(rsem, f"one{n}", blk.at[0, pl.ds(0, SIDE - 1), 0])

        @pl.when(core == 0)
        def _():
            for i in (1, SIDE - 1):
                part = blk.at[cy, :, 0]
                copy(f"two{n}", part, part, (b, lax.rem(cy + i, SIDE) * SIDE + cx)).start()

        @pl.when(core == 1)
        def _():
            for i in (1, SIDE - 1):
                part = blk.at[:, cx, 1]
                copy(f"two{n}", part, part, (b, cy * SIDE + lax.rem(cx + i, SIDE))).start()

        drains.append(lambda: wait_bytes(ssem, f"two{n}", blk.at[pl.ds(0, 2), :, 0]))

    def step2b(n):
        blk = blocks[n]
        wait_bytes(rsem, f"two{n}", blk.at[pl.ds(0, 2), :, 0])

        @pl.when(core == 0)
        def _():
            for i in (1, SIDE - 1):
                part = blk.at[lax.rem(cy + SIDE - i, SIDE), pl.ds(i // 2 * 2, 2), 0]
                copy(f"far{n}", part, part, (b, lax.rem(cy + i, SIDE) * SIDE + cx)).start()

        @pl.when(core == 1)
        def _():
            for i in (1, SIDE - 1):
                part = blk.at[pl.ds(i // 2 * 2, 2), lax.rem(cx + SIDE - i, SIDE), 1]
                copy(f"far{n}", part, part, (b, cy * SIDE + lax.rem(cx + i, SIDE))).start()

        drains.append(lambda: wait_bytes(ssem, f"far{n}", blk.at[0, :, 0]))

    def step3(n):
        blk = blocks[n]
        wait_bytes(rsem, f"far{n}", blk.at[0, :, 0])
        part = blk.at[:, :, core]
        copy(f"three{n}", part, part, (b + 1 - 2 * core, c)).start()
        drains.append(lambda: wait_bytes(ssem, f"three{n}", blk.at[:, :, 0]))

    def step4(n):
        wait_bytes(rsem, f"three{n}", blocks[n].at[:, :, 0])

    step1(0)

    def spread(buf, dst):
        for q in range(G // 2):
            even, odd = mix_halves(buf[2 * q].astype(F32), buf[2 * q + 1].astype(F32))
            lanes = pl.ds(q * PAIR, PAIR)
            dst[pl.ds(0, G), lanes] = even.astype(dst.dtype)
            dst[pl.ds(G, G), lanes] = odd.astype(dst.dtype)

    def decay_scales():
        arrived("dec", dall)
        a = dall[...].reshape(FRAMES, PAIR)
        later = lax.broadcasted_iota(jnp.int32, (FRAMES, FRAMES), 0)
        earlier = lax.broadcasted_iota(jnp.int32, (FRAMES, FRAMES), 1)
        logs = jnp.dot(
            (earlier <= later).astype(F32), jnp.log(a), precision=HI, preferred_element_type=F32
        )
        for l in range(LAYERS):
            left = left_half((FRAMES, PAIR))
            mine = left if l == 0 else jnp.logical_not(left)
            la = jnp.where(mine, logs, pltpu.roll(logs, HALF, 1))
            da = 1.0 - jnp.where(mine, a, pltpu.roll(a, HALF, 1))
            for t in range(FRAMES // CHUNK):
                rows = slice(t * CHUNK, (t + 1) * CHUNK)
                rel = la[rows] - la[t * CHUNK + CHUNK // 2 - 1 : t * CHUNK + CHUNK // 2]
                scale_e[l, pl.ds(t * CHUNK, CHUNK)] = jnp.exp(rel)
                scale_w[l, pl.ds(t * CHUNK, CHUNK)] = da[rows] * jnp.exp(-rel)
            end = la[CHUNK - 1 : CHUNK]
            scale_x[l] = da[:CHUNK] * jnp.exp(end - la[:CHUNK])
            scale_f[l] = jnp.exp(la[CHUNK:] - end)

    arrived("x", buf_x)
    spread(buf_x, xs)

    for layer in range(LAYERS):

        def named(name, layer=layer):
            return f"{name}{layer}"

        mixed32 = jnp.dot(aperm[layer], xs[...], precision=HI, preferred_element_type=F32)
        mixed = mixed32.astype(BF16)
        mixed32 = mixed.astype(F32)
        for q in range(G // 2):
            lanes = slice(q * PAIR, (q + 1) * PAIR)
            pieces = mix_halves(mixed32[:G, lanes], mixed32[G:, lanes])
            for i in range(2):
                send_a[layer, 2 * q + i] = pieces[i].astype(BF16)
        send("mp", named("a"), lambda peer: send_a.at[layer, peer], buf_a.at[layer])
        buf_a[layer, c] = send_a[layer, c]
        if layer == 0:
            wait_bytes(rsem, "wb0", flat_wb0)
            weights = wb0[...].reshape(WIDE, PAIR)
        else:
            weights = blk0[:, :, :, :, pl.ds(WIDE, PAIR)].reshape(WIDE, PAIR)
        coef = jnp.dot(mixed, weights, preferred_element_type=F32)
        in_b, out_c = mix_halves(coef[:G], coef[G:])
        for pair in range(USED):
            send_k[layer, pair, :, pl.ds(0, PAIR)] = in_b[pair : pair + 1]
            send_k[layer, pair, :, pl.ds(PAIR, PAIR)] = out_c[pair : pair + 1]
        send_used(named("k"), lambda peer: send_k.at[layer, peer], buf_k.at[layer])

        if layer == 0:
            step2(0)
        arrived(named("a"), buf_a.at[layer])
        tmp[0] = buf_a[layer].reshape(FRAMES, PAIR).astype(F32)
        for pair in range(USED):
            send_b[layer, pair] = tmp[0, pl.ds(pair, G, stride=G), :].astype(BF16)
        send_used(named("b"), lambda peer: send_b.at[layer, peer], buf_b.at[layer])

        @pl.when(scans)
        def _():
            buf_b[layer, b] = send_b[layer, b]
            buf_k[layer, b] = send_k[layer, b]
            arrived(named("k"), buf_k.at[layer])
            for block in range(G):
                for part in range(2):
                    tmp[1 + part, pl.ds(block, 1)] = buf_k[layer, block, :, pl.ds(part * PAIR, PAIR)]
            for part in range(2):
                send_g[layer, :, pl.ds(part * PAIR, PAIR)] = tmp[1 + part, pl.ds(0, G)].astype(BF16)
            peers(
                "mp",
                lambda peer: copy(
                    named("g"), send_g.at[layer], buf_g.at[layer, c], (b, peer)
                ).start(),
            )
            buf_g[layer, c] = send_g[layer]

        def drain_g(layer=layer):
            @pl.when(scans)
            def _():
                wait_bytes(ssem, f"g{layer}", buf_g.at[layer, pl.ds(0, G - 1)])

        drains.append(drain_g)
        if layer == 0:
            step2b(0)
        if layer == 1:
            step2b(1)
        if layer == 0:
            decay_scales()

        @pl.when(scans)
        def _():
            arrived(named("g"), buf_g.at[layer])
            for part in range(2):
                tmp[1 + part] = buf_g[layer, :, :, pl.ds(part * PAIR, PAIR)].reshape(FRAMES, PAIR).astype(F32)
            bp, cp = [
                jnp.concatenate([tmp[1 + part, pl.ds(k, G, stride=G), :] for k in range(G)], axis=0)
                for part in range(2)
            ]
            bp = bp.astype(BF16)
            left = left_half((FRAMES, PAIR))
            causal = lax.broadcasted_iota(jnp.int32, (CHUNK, CHUNK), 1) <= lax.broadcasted_iota(
                jnp.int32, (CHUNK, CHUNK), 0
            )

            def grid(cj, bj, masked):
                g = lax.dot_general(
                    cj, bj, (((1,), (1,)), ((), ())), preferred_element_type=F32
                )
                return (jnp.where(causal, g, 0.0) if masked else g).astype(BF16)

            grids = []
            for j in range(2):
                cj = jnp.where(left if j == 0 else jnp.logical_not(left), cp, 0.0).astype(BF16)
                grids.append(
                    (
                        grid(cj[:CHUNK], bp[:CHUNK], True),
                        grid(cj[CHUNK:], bp[CHUNK:], True),
                        grid(cj[CHUNK:], bp[:CHUNK], False),
                    )
                )
            arrived(named("b"), buf_b.at[layer])
            m = buf_b[layer].reshape(FRAMES, PAIR).astype(F32)
            v = (m * scale_w[layer]).astype(BF16)
            vx = (m[:CHUNK] * scale_x[layer]).astype(BF16)
            values = (v[:CHUNK], v[CHUNK:], vx)
            y0, y1, yx = [
                jnp.where(
                    left[:CHUNK],
                    jnp.dot(grids[0][i], values[i], preferred_element_type=F32),
                    jnp.dot(grids[1][i], values[i], preferred_element_type=F32),
                )
                for i in range(3)
            ]
            gain = skip[pl.ds(layer, 1), :]
            gain = jnp.concatenate([gain, gain], axis=1)
            low = y0 * scale_e[layer, pl.ds(0, CHUNK)] + gain * m[:CHUNK]
            high = (
                y1 * scale_e[layer, pl.ds(CHUNK, CHUNK)] + yx * scale_f[layer] + gain * m[CHUNK:]
            )
            send_c[layer, pl.ds(0, G // 2)] = low.astype(BF16).reshape(G // 2, G, PAIR)
            send_c[layer, pl.ds(G // 2, G // 2)] = high.astype(BF16).reshape(G // 2, G, PAIR)
            peers(
                "frames",
                lambda peer: copy(
                    named("c"), send_c.at[layer, peer], buf_c.at[layer, b], (peer, c)
                ).start(),
            )
            buf_c[layer, b] = send_c[layer, b]

        def drain_c(layer=layer):
            @pl.when(scans)
            def _():
                wait_bytes(ssem, f"c{layer}", buf_c.at[layer, pl.ds(0, G - 1)])

        drains.append(drain_c)
        if layer == 0:
            step3(0)
        if layer == 0:
            step1(1)
        if layer == 1:
            step3(1)

        @pl.when(scans)
        def _():
            wait_bytes(rsem, named("c"), buf_c.at[layer, pl.ds(0, USED - 1)])

        @pl.when(jnp.logical_not(scans))
        def _():
            wait_bytes(rsem, named("c"), buf_c.at[layer, pl.ds(0, USED)])

        tmp[0] = buf_c[layer].reshape(FRAMES, PAIR).astype(F32)
        for frame in range(G):
            send_d[layer, frame] = tmp[0, pl.ds(frame, G, stride=G), :].astype(BF16)
        send("mp", named("d"), lambda peer: send_d.at[layer, peer], buf_d.at[layer])
        buf_d[layer, c] = send_d[layer, c]
        if layer == 0:
            step2(1)

        if layer == 0:
            step4(0)
        if layer == 1:
            step4(1)
        arrived(named("d"), buf_d.at[layer])
        spread(buf_d.at[layer], res)
        weights = blocks[layer][:, :, :, :, pl.ds(0, WIDE)].reshape(WIDE, WIDE)
        xs[...] += jnp.dot(res[...], weights, preferred_element_type=F32)

    for q in range(G // 2):
        lanes = pl.ds(q * PAIR, PAIR)
        pieces = mix_halves(xs[pl.ds(0, G), lanes], xs[pl.ds(G, G), lanes])
        send_e[2 * q] = pieces[0]
        send_e[2 * q + 1] = pieces[1]
    send("mp", "e", lambda peer: send_e.at[peer], buf_e)
    buf_e[c] = send_e[c]
    for drain in drains:
        drain()
    arrived("e", buf_e)
    out_ref[...] = buf_e[...]


def shards(motion, adjacency, w_bc, decay, skip, w_out):
    vm = pltpu.VMEM
    part = HALF // 2
    out = pl.pallas_call(
        body,
        out_shape=jax.ShapeDtypeStruct((G, G, PAIR), F32),
        in_specs=[pl.BlockSpec(memory_space=pltpu.HBM)] * 6,
        out_specs=pl.BlockSpec(memory_space=vm),
        scratch_shapes=[
            vm((JOINTS, G, HALF), BF16),
            vm((JOINTS, LAYERS, JOINTS), F32),
            vm((LAYERS, JOINTS, JOINTS), F32),
            vm((LAYERS, G, HALF), F32),
            vm((LAYERS, HALF), F32),
            vm((SIDE, SIDE, 2, part, PAIR), BF16),
            vm((SIDE, SIDE, 2, part, WIDE + PAIR), BF16),
            vm((SIDE, SIDE, 2, part, WIDE), BF16),
            vm((G, PAIR), F32),
            vm((G, G, PAIR), F32),
            vm((LAYERS, FRAMES, PAIR), F32),
            vm((LAYERS, FRAMES, PAIR), F32),
            vm((LAYERS, CHUNK, PAIR), F32),
            vm((LAYERS, CHUNK, PAIR), F32),
            vm((LAYERS, 2 * G, 2 * G), F32),
            vm((G, G, PAIR), BF16),
            vm((G, G, PAIR), BF16),
            vm((LAYERS, G, G, PAIR), BF16),
            vm((LAYERS, G, G, PAIR), BF16),
            vm((LAYERS, USED, 1, 2 * PAIR), F32),
            vm((LAYERS, G, 1, 2 * PAIR), F32),
            vm((LAYERS, G, 2 * PAIR), BF16),
            vm((LAYERS, G, G, 2 * PAIR), BF16),
            vm((LAYERS, USED, G, PAIR), BF16),
            vm((LAYERS, G, G, PAIR), BF16),
            vm((LAYERS, G, G, PAIR), BF16),
            vm((LAYERS, G, G, PAIR), BF16),
            vm((LAYERS, G, G, PAIR), BF16),
            vm((LAYERS, G, G, PAIR), BF16),
            vm((G, G, PAIR), F32),
            vm((G, G, PAIR), F32),
            vm((3, FRAMES, PAIR), F32),
            vm((2 * G, WIDE), F32),
            vm((2 * G, WIDE), BF16),
            pltpu.SemaphoreType.DMA((8,)),
            pltpu.SemaphoreType.DMA((24,)),
            pltpu.SemaphoreType.DMA((24,)),
        ],
        compiler_params=pltpu.CompilerParams(
            collective_id=0, has_side_effects=True, vmem_limit_bytes=56 * 2**20
        ),
    )(
        motion.transpose(1, 0, 2),
        adjacency.transpose(1, 0, 2),
        w_bc.reshape(LAYERS, 2, part, PAIR),
        decay,
        skip,
        w_out.reshape(LAYERS, 2, part, WIDE),
    )
    return out.reshape(G, 2 * G, HALF)[:, :JOINTS]


def solution(mesh):
    return jax.shard_map(
        shards,
        mesh=mesh,
        in_specs=(
            P("frames", None, "mp"),
            P(),
            P(None, "mp", None),
            P(None, "frames", "mp"),
            P(None, "mp"),
            P(None, "mp", None),
        ),
        out_specs=P("frames", None, "mp"),
        check_vma=False,
    )
```

```python
import jax
import jax.numpy as jnp
from jax import lax
from jax.experimental import pallas as pl
from jax.experimental.pallas import tpu as pltpu
from jax.sharding import PartitionSpec as P

MESH = pl.DeviceIdType.MESH
HI = lax.Precision.HIGHEST
F32, BF16 = jnp.float32, jnp.bfloat16
LAYERS = 2
JOINTS = 25
G = 16
SIDE = 4
USED = 13
HALF, PAIR = 64, 128
WIDE = G * HALF
FRAMES = 256
CHUNK = 128


def left_half(shape):
    return lax.broadcasted_iota(jnp.int32, shape, len(shape) - 1) % PAIR < HALF


def mix_halves(first, second):
    left = left_half(first.shape)
    return (
        jnp.where(left, first, pltpu.roll(second, HALF, 1)),
        jnp.where(left, pltpu.roll(first, HALF, 1), second),
    )


def body(
    x_hbm, a_hbm, wbc_hbm, dec_hbm, skip_hbm, wout_hbm, out_ref,
    xin, araw, ain, din, skip, wb0, blk0, blk1, dsend, dall,
    scale_e, scale_w, scale_x, scale_f, aperm,
    send_x, buf_x, send_a, buf_a, send_k, buf_k, send_g, buf_g,
    send_b, buf_b, send_c, buf_c, send_d, buf_d, send_e, buf_e,
    tmp, xs, res, lsem, ssem, rsem,
):
    b, c = lax.axis_index("frames"), lax.axis_index("mp")
    core = lax.rem(b, 2)
    cy, cx = c // SIDE, lax.rem(c, SIDE)
    scans = b < USED

    loads = {}

    def load(name, src, dst):
        loads[name] = pltpu.make_async_copy(src, dst, lsem.at[len(loads)])
        loads[name].start()

    load("x", x_hbm, xin)
    load("wb0", wbc_hbm.at[0], wb0.at[cy, cx])
    load("dec", dec_hbm, din)
    load("a", a_hbm, araw)
    load("skip", skip_hbm, skip)
    load("out0", wout_hbm.at[0, core], blk0.at[cy, cx, core, :, pl.ds(0, WIDE)])
    load("bc1", wbc_hbm.at[1, core], blk0.at[cy, cx, core, :, pl.ds(WIDE, PAIR)])
    load("out1", wout_hbm.at[1, core], blk1.at[cy, cx, core])

    def at(axis, peer):
        return (b, peer) if axis == "mp" else (peer, c)

    def peers(axis, act):
        def off(k, half):
            return half + (k + 1) // 2 * (1 - 2 * lax.rem(k + 1, 2))

        def one(k, carry):
            if axis == "mp":
                to_y = lax.rem(cy + off(k // SIDE, SIDE // 2), SIDE)
                to_x = lax.rem(cx + off(lax.rem(k, SIDE), SIDE // 2), SIDE)
                act(to_y * SIDE + to_x)
            else:
                act(lax.rem(b + off(k, G // 2), G))
            return carry

        lax.fori_loop(0, G - 1, one, 0)

    names = []

    def number(name):
        if name not in names:
            names.append(name)
        return names.index(name)

    def copy(name, src, dst, device):
        return pltpu.make_async_remote_copy(
            src_ref=src,
            dst_ref=dst,
            send_sem=ssem.at[number(name)],
            recv_sem=rsem.at[number(name)],
            device_id=device,
            device_id_type=MESH,
        )

    def wait_bytes(sem, name, ref):
        pltpu.make_async_copy(ref, ref, sem.at[number(name)]).wait()

    drains = []

    def send(axis, name, src, dst):
        me = c if axis == "mp" else b
        peers(axis, lambda peer: copy(name, src(peer), dst.at[me], at(axis, peer)).start())
        drains.append(lambda: wait_bytes(ssem, name, dst.at[pl.ds(0, G - 1)]))

    def send_used(name, src, dst):
        def act(peer):
            @pl.when(peer < USED)
            def _():
                copy(name, src(peer), dst.at[b], (peer, c)).start()

        peers("frames", act)

        def drain():
            @pl.when(scans)
            def _():
                wait_bytes(ssem, name, dst.at[pl.ds(0, USED - 1)])

            @pl.when(jnp.logical_not(scans))
            def _():
                wait_bytes(ssem, name, dst.at[pl.ds(0, USED)])

        drains.append(drain)

    def arrived(name, dst):
        wait_bytes(rsem, name, dst.at[pl.ds(0, G - 1)])

    barrier = pltpu.get_barrier_semaphore()
    for axis in ("frames", "mp"):
        peers(
            axis,
            lambda peer, axis=axis: pl.semaphore_signal(
                barrier, inc=1, device_id=at(axis, peer), device_id_type=MESH
            ),
        )

    loads["x"].wait()
    for pair in range(G):
        if pair < USED:
            even = xin[2 * pair].astype(F32)
            odd = xin[2 * pair + 1].astype(F32) if 2 * pair + 1 < JOINTS else jnp.zeros_like(even)
            tmp[0, pl.ds(pair * G, G)] = jnp.concatenate([even, odd], axis=1)
        else:
            tmp[0, pl.ds(pair * G, G)] = jnp.zeros((G, PAIR), F32)
    for frame in range(G):
        send_x[frame] = tmp[0, pl.ds(frame, G, stride=G), :].astype(BF16)
    buf_x[c] = send_x[c]

    pl.semaphore_wait(barrier, 2 * (G - 1))

    send("mp", "x", lambda peer: send_x.at[peer], buf_x)
    loads["wb0"].wait()
    peers("mp", lambda peer: copy("wb0", wb0.at[cy, cx], wb0.at[cy, cx], at("mp", peer)).start())
    flat_wb0 = wb0.reshape(G, 2, HALF // 2, PAIR).at[pl.ds(0, G - 1)]
    drains.append(lambda: wait_bytes(ssem, "wb0", flat_wb0))
    loads["dec"].wait()
    dsend[...] = jnp.concatenate([din[0], din[1]], axis=1)
    send("frames", "dec", lambda peer: dsend, dall)
    dall[b] = dsend[...]
    loads["a"].wait()
    for joint in range(JOINTS):
        for layer in range(LAYERS):
            ain[layer, pl.ds(joint, 1)] = araw[joint, pl.ds(layer, 1)]
    row = lax.broadcasted_iota(jnp.int32, (2 * G, JOINTS), 0)
    pick = (lax.broadcasted_iota(jnp.int32, (2 * G, JOINTS), 1) == 2 * lax.rem(row, G) + row // G).astype(F32)
    for layer in range(LAYERS):
        half = jnp.dot(pick, ain[layer], precision=HI, preferred_element_type=F32)
        aperm[layer] = lax.dot_general(
            half, pick, (((1,), (1,)), ((), ())), precision=HI, preferred_element_type=F32
        )
        buf_c[layer, pl.ds(USED, G - USED)] = jnp.zeros((G - USED, G, PAIR), BF16)
    for name in ("skip", "out0", "bc1", "out1"):
        loads[name].wait()

    blocks = (blk0, blk1)

    def step1(n):
        blk = blocks[n]
        for i in range(1, SIDE):
            to = lax.rem(cy + i * core, SIDE) * SIDE + lax.rem(cx + i * (1 - core), SIDE)
            part = blk.at[cy, cx, core]
            copy(f"one{n}", part, part, (b, to)).start()
        drains.append(lambda: wait_bytes(ssem, f"one{n}", blk.at[0, pl.ds(0, SIDE - 1), 0]))

    def step2(n):
        blk = blocks[n]
        wait_bytes(rsem, f"one{n}", blk.at[0, pl.ds(0, SIDE - 1), 0])

        @pl.when(core == 0)
        def _():
            for i in (1, SIDE - 1):
                part = blk.at[cy, :, 0]
                copy(f"two{n}", part, part, (b, lax.rem(cy + i, SIDE) * SIDE + cx)).start()

        @pl.when(core == 1)
        def _():
            for i in (1, SIDE - 1):
                part = blk.at[:, cx, 1]
                copy(f"two{n}", part, part, (b, cy * SIDE + lax.rem(cx + i, SIDE))).start()

        drains.append(lambda: wait_bytes(ssem, f"two{n}", blk.at[pl.ds(0, 2), :, 0]))

    def step2b(n):
        blk = blocks[n]
        wait_bytes(rsem, f"two{n}", blk.at[pl.ds(0, 2), :, 0])

        @pl.when(core == 0)
        def _():
            for i in (1, SIDE - 1):
                part = blk.at[lax.rem(cy + SIDE - i, SIDE), pl.ds(i // 2 * 2, 2), 0]
                copy(f"far{n}", part, part, (b, lax.rem(cy + i, SIDE) * SIDE + cx)).start()

        @pl.when(core == 1)
        def _():
            for i in (1, SIDE - 1):
                part = blk.at[pl.ds(i // 2 * 2, 2), lax.rem(cx + SIDE - i, SIDE), 1]
                copy(f"far{n}", part, part, (b, cy * SIDE + lax.rem(cx + i, SIDE))).start()

        drains.append(lambda: wait_bytes(ssem, f"far{n}", blk.at[0, :, 0]))

    def step3(n):
        blk = blocks[n]
        wait_bytes(rsem, f"far{n}", blk.at[0, :, 0])
        part = blk.at[:, :, core]
        copy(f"three{n}", part, part, (b + 1 - 2 * core, c)).start()
        drains.append(lambda: wait_bytes(ssem, f"three{n}", blk.at[:, :, 0]))

    def step4(n):
        wait_bytes(rsem, f"three{n}", blocks[n].at[:, :, 0])

    step1(0)
    step1(1)

    def spread(buf, dst):
        for q in range(G // 2):
            even, odd = mix_halves(buf[2 * q].astype(F32), buf[2 * q + 1].astype(F32))
            lanes = pl.ds(q * PAIR, PAIR)
            dst[pl.ds(0, G), lanes] = even.astype(dst.dtype)
            dst[pl.ds(G, G), lanes] = odd.astype(dst.dtype)

    def decay_scales():
        arrived("dec", dall)
        a = dall[...].reshape(FRAMES, PAIR)
        later = lax.broadcasted_iota(jnp.int32, (FRAMES, FRAMES), 0)
        earlier = lax.broadcasted_iota(jnp.int32, (FRAMES, FRAMES), 1)
        logs = jnp.dot(
            (earlier <= later).astype(F32), jnp.log(a), precision=HI, preferred_element_type=F32
        )
        for l in range(LAYERS):
            left = left_half((FRAMES, PAIR))
            mine = left if l == 0 else jnp.logical_not(left)
            la = jnp.where(mine, logs, pltpu.roll(logs, HALF, 1))
            da = 1.0 - jnp.where(mine, a, pltpu.roll(a, HALF, 1))
            for t in range(FRAMES // CHUNK):
                rows = slice(t * CHUNK, (t + 1) * CHUNK)
                rel = la[rows] - la[t * CHUNK + CHUNK // 2 - 1 : t * CHUNK + CHUNK // 2]
                scale_e[l, pl.ds(t * CHUNK, CHUNK)] = jnp.exp(rel)
                scale_w[l, pl.ds(t * CHUNK, CHUNK)] = da[rows] * jnp.exp(-rel)
            end = la[CHUNK - 1 : CHUNK]
            scale_x[l] = da[:CHUNK] * jnp.exp(end - la[:CHUNK])
            scale_f[l] = jnp.exp(la[CHUNK:] - end)

    arrived("x", buf_x)
    spread(buf_x, xs)

    for layer in range(LAYERS):

        def named(name, layer=layer):
            return f"{name}{layer}"

        mixed32 = jnp.dot(aperm[layer], xs[...], precision=HI, preferred_element_type=F32)
        mixed = mixed32.astype(BF16)
        mixed32 = mixed.astype(F32)
        for q in range(G // 2):
            lanes = slice(q * PAIR, (q + 1) * PAIR)
            pieces = mix_halves(mixed32[:G, lanes], mixed32[G:, lanes])
            for i in range(2):
                send_a[layer, 2 * q + i] = pieces[i].astype(BF16)
        send("mp", named("a"), lambda peer: send_a.at[layer, peer], buf_a.at[layer])
        buf_a[layer, c] = send_a[layer, c]
        if layer == 1:
            step2(1)
        if layer == 0:
            wait_bytes(rsem, "wb0", flat_wb0)
            weights = wb0[...].reshape(WIDE, PAIR)
        else:
            weights = blk0[:, :, :, :, pl.ds(WIDE, PAIR)].reshape(WIDE, PAIR)
        coef = jnp.dot(mixed, weights, preferred_element_type=F32)
        in_b, out_c = mix_halves(coef[:G], coef[G:])
        for pair in range(USED):
            send_k[layer, pair, :, pl.ds(0, PAIR)] = in_b[pair : pair + 1]
            send_k[layer, pair, :, pl.ds(PAIR, PAIR)] = out_c[pair : pair + 1]
        send_used(named("k"), lambda peer: send_k.at[layer, peer], buf_k.at[layer])

        if layer == 0:
            step2(0)
        arrived(named("a"), buf_a.at[layer])
        tmp[0] = buf_a[layer].reshape(FRAMES, PAIR).astype(F32)
        for pair in range(USED):
            send_b[layer, pair] = tmp[0, pl.ds(pair, G, stride=G), :].astype(BF16)
        send_used(named("b"), lambda peer: send_b.at[layer, peer], buf_b.at[layer])

        @pl.when(scans)
        def _():
            buf_b[layer, b] = send_b[layer, b]
            buf_k[layer, b] = send_k[layer, b]
            arrived(named("k"), buf_k.at[layer])
            for block in range(G):
                for part in range(2):
                    tmp[1 + part, pl.ds(block, 1)] = buf_k[layer, block, :, pl.ds(part * PAIR, PAIR)]
            for part in range(2):
                send_g[layer, :, pl.ds(part * PAIR, PAIR)] = tmp[1 + part, pl.ds(0, G)].astype(BF16)
            peers(
                "mp",
                lambda peer: copy(
                    named("g"), send_g.at[layer], buf_g.at[layer, c], (b, peer)
                ).start(),
            )
            buf_g[layer, c] = send_g[layer]

        def drain_g(layer=layer):
            @pl.when(scans)
            def _():
                wait_bytes(ssem, f"g{layer}", buf_g.at[layer, pl.ds(0, G - 1)])

        drains.append(drain_g)
        if layer == 0:
            step2b(0)
        if layer == 1:
            step2b(1)
        if layer == 0:
            decay_scales()

        @pl.when(scans)
        def _():
            arrived(named("g"), buf_g.at[layer])
            for part in range(2):
                tmp[1 + part] = buf_g[layer, :, :, pl.ds(part * PAIR, PAIR)].reshape(FRAMES, PAIR).astype(F32)
            bp, cp = [
                jnp.concatenate([tmp[1 + part, pl.ds(k, G, stride=G), :] for k in range(G)], axis=0)
                for part in range(2)
            ]
            bp = bp.astype(BF16)
            left = left_half((FRAMES, PAIR))
            causal = lax.broadcasted_iota(jnp.int32, (CHUNK, CHUNK), 1) <= lax.broadcasted_iota(
                jnp.int32, (CHUNK, CHUNK), 0
            )

            def grid(cj, bj, masked):
                g = lax.dot_general(
                    cj, bj, (((1,), (1,)), ((), ())), preferred_element_type=F32
                )
                return (jnp.where(causal, g, 0.0) if masked else g).astype(BF16)

            grids = []
            for j in range(2):
                cj = jnp.where(left if j == 0 else jnp.logical_not(left), cp, 0.0).astype(BF16)
                grids.append(
                    (
                        grid(cj[:CHUNK], bp[:CHUNK], True),
                        grid(cj[CHUNK:], bp[CHUNK:], True),
                        grid(cj[CHUNK:], bp[:CHUNK], False),
                    )
                )
            arrived(named("b"), buf_b.at[layer])
            m = buf_b[layer].reshape(FRAMES, PAIR).astype(F32)
            v = (m * scale_w[layer]).astype(BF16)
            vx = (m[:CHUNK] * scale_x[layer]).astype(BF16)
            values = (v[:CHUNK], v[CHUNK:], vx)
            y0, y1, yx = [
                jnp.where(
                    left[:CHUNK],
                    jnp.dot(grids[0][i], values[i], preferred_element_type=F32),
                    jnp.dot(grids[1][i], values[i], preferred_element_type=F32),
                )
                for i in range(3)
            ]
            gain = skip[pl.ds(layer, 1), :]
            gain = jnp.concatenate([gain, gain], axis=1)
            low = y0 * scale_e[layer, pl.ds(0, CHUNK)] + gain * m[:CHUNK]
            high = (
                y1 * scale_e[layer, pl.ds(CHUNK, CHUNK)] + yx * scale_f[layer] + gain * m[CHUNK:]
            )
            send_c[layer, pl.ds(0, G // 2)] = low.astype(BF16).reshape(G // 2, G, PAIR)
            send_c[layer, pl.ds(G // 2, G // 2)] = high.astype(BF16).reshape(G // 2, G, PAIR)
            peers(
                "frames",
                lambda peer: copy(
                    named("c"), send_c.at[layer, peer], buf_c.at[layer, b], (peer, c)
                ).start(),
            )
            buf_c[layer, b] = send_c[layer, b]

        def drain_c(layer=layer):
            @pl.when(scans)
            def _():
                wait_bytes(ssem, f"c{layer}", buf_c.at[layer, pl.ds(0, G - 1)])

        drains.append(drain_c)
        if layer == 0:
            step3(0)
        if layer == 1:
            step3(1)

        @pl.when(scans)
        def _():
            wait_bytes(rsem, named("c"), buf_c.at[layer, pl.ds(0, USED - 1)])

        @pl.when(jnp.logical_not(scans))
        def _():
            wait_bytes(rsem, named("c"), buf_c.at[layer, pl.ds(0, USED)])

        tmp[0] = buf_c[layer].reshape(FRAMES, PAIR).astype(F32)
        for frame in range(G):
            send_d[layer, frame] = tmp[0, pl.ds(frame, G, stride=G), :].astype(BF16)
        send("mp", named("d"), lambda peer: send_d.at[layer, peer], buf_d.at[layer])
        buf_d[layer, c] = send_d[layer, c]

        if layer == 0:
            step4(0)
        if layer == 1:
            step4(1)
        arrived(named("d"), buf_d.at[layer])
        spread(buf_d.at[layer], res)
        weights = blocks[layer][:, :, :, :, pl.ds(0, WIDE)].reshape(WIDE, WIDE)
        xs[...] += jnp.dot(res[...], weights, preferred_element_type=F32)

    for q in range(G // 2):
        lanes = pl.ds(q * PAIR, PAIR)
        pieces = mix_halves(xs[pl.ds(0, G), lanes], xs[pl.ds(G, G), lanes])
        send_e[2 * q] = pieces[0]
        send_e[2 * q + 1] = pieces[1]
    send("mp", "e", lambda peer: send_e.at[peer], buf_e)
    buf_e[c] = send_e[c]
    for drain in drains:
        drain()
    arrived("e", buf_e)
    out_ref[...] = buf_e[...]


def shards(motion, adjacency, w_bc, decay, skip, w_out):
    vm = pltpu.VMEM
    part = HALF // 2
    out = pl.pallas_call(
        body,
        out_shape=jax.ShapeDtypeStruct((G, G, PAIR), F32),
        in_specs=[pl.BlockSpec(memory_space=pltpu.HBM)] * 6,
        out_specs=pl.BlockSpec(memory_space=vm),
        scratch_shapes=[
            vm((JOINTS, G, HALF), BF16),
            vm((JOINTS, LAYERS, JOINTS), F32),
            vm((LAYERS, JOINTS, JOINTS), F32),
            vm((LAYERS, G, HALF), F32),
            vm((LAYERS, HALF), F32),
            vm((SIDE, SIDE, 2, part, PAIR), BF16),
            vm((SIDE, SIDE, 2, part, WIDE + PAIR), BF16),
            vm((SIDE, SIDE, 2, part, WIDE), BF16),
            vm((G, PAIR), F32),
            vm((G, G, PAIR), F32),
            vm((LAYERS, FRAMES, PAIR), F32),
            vm((LAYERS, FRAMES, PAIR), F32),
            vm((LAYERS, CHUNK, PAIR), F32),
            vm((LAYERS, CHUNK, PAIR), F32),
            vm((LAYERS, 2 * G, 2 * G), F32),
            vm((G, G, PAIR), BF16),
            vm((G, G, PAIR), BF16),
            vm((LAYERS, G, G, PAIR), BF16),
            vm((LAYERS, G, G, PAIR), BF16),
            vm((LAYERS, USED, 1, 2 * PAIR), F32),
            vm((LAYERS, G, 1, 2 * PAIR), F32),
            vm((LAYERS, G, 2 * PAIR), BF16),
            vm((LAYERS, G, G, 2 * PAIR), BF16),
            vm((LAYERS, USED, G, PAIR), BF16),
            vm((LAYERS, G, G, PAIR), BF16),
            vm((LAYERS, G, G, PAIR), BF16),
            vm((LAYERS, G, G, PAIR), BF16),
            vm((LAYERS, G, G, PAIR), BF16),
            vm((LAYERS, G, G, PAIR), BF16),
            vm((G, G, PAIR), F32),
            vm((G, G, PAIR), F32),
            vm((3, FRAMES, PAIR), F32),
            vm((2 * G, WIDE), F32),
            vm((2 * G, WIDE), BF16),
            pltpu.SemaphoreType.DMA((8,)),
            pltpu.SemaphoreType.DMA((24,)),
            pltpu.SemaphoreType.DMA((24,)),
        ],
        compiler_params=pltpu.CompilerParams(
            collective_id=0, has_side_effects=True, vmem_limit_bytes=56 * 2**20
        ),
    )(
        motion.transpose(1, 0, 2),
        adjacency.transpose(1, 0, 2),
        w_bc.reshape(LAYERS, 2, part, PAIR),
        decay,
        skip,
        w_out.reshape(LAYERS, 2, part, WIDE),
    )
    return out.reshape(G, 2 * G, HALF)[:, :JOINTS]


def solution(mesh):
    return jax.shard_map(
        shards,
        mesh=mesh,
        in_specs=(
            P("frames", None, "mp"),
            P(),
            P(None, "mp", None),
            P(None, "frames", "mp"),
            P(None, "mp"),
            P(None, "mp", None),
        ),
        out_specs=P("frames", None, "mp"),
        check_vma=False,
    )
```

```python
import jax
import jax.numpy as jnp
from jax import lax
from jax.experimental import pallas as pl
from jax.experimental.pallas import tpu as pltpu
from jax.sharding import PartitionSpec as P

MESH = pl.DeviceIdType.MESH
HI = lax.Precision.HIGHEST
F32, BF16 = jnp.float32, jnp.bfloat16
LAYERS = 2
JOINTS = 25
G = 16
SIDE = 4
USED = 13
HALF, PAIR = 64, 128
WIDE = G * HALF
FRAMES = 256
CHUNK = 128


def left_half(shape):
    return lax.broadcasted_iota(jnp.int32, shape, len(shape) - 1) % PAIR < HALF


def mix_halves(first, second):
    left = left_half(first.shape)
    return (
        jnp.where(left, first, pltpu.roll(second, HALF, 1)),
        jnp.where(left, pltpu.roll(first, HALF, 1), second),
    )


def body(
    x_hbm, a_hbm, wbc_hbm, dec_hbm, skip_hbm, wout_hbm, out_ref,
    xin, araw, ain, din, skip, wb0, blk0, blk1, dsend, dall,
    scale_e, scale_w, scale_x, scale_f, aperm,
    send_x, buf_x, send_a, buf_a, send_k, buf_k, send_g, buf_g,
    send_b, buf_b, send_c, buf_c, send_d, buf_d, send_e, buf_e,
    tmp, xs, res, lsem, ssem, rsem,
):
    b, c = lax.axis_index("frames"), lax.axis_index("mp")
    core = lax.rem(b, 2)
    cy, cx = c // SIDE, lax.rem(c, SIDE)
    scans = b < USED

    loads = {}

    def load(name, src, dst):
        loads[name] = pltpu.make_async_copy(src, dst, lsem.at[len(loads)])
        loads[name].start()

    load("x", x_hbm, xin)

    def at(axis, peer):
        return (b, peer) if axis == "mp" else (peer, c)

    def peers(axis, act):
        def off(k, half):
            return half + (k + 1) // 2 * (1 - 2 * lax.rem(k + 1, 2))

        def one(k, carry):
            if axis == "mp":
                to_y = lax.rem(cy + off(k // SIDE, SIDE // 2), SIDE)
                to_x = lax.rem(cx + off(lax.rem(k, SIDE), SIDE // 2), SIDE)
                act(to_y * SIDE + to_x)
            else:
                act(lax.rem(b + off(k, G // 2), G))
            return carry

        lax.fori_loop(0, G - 1, one, 0)

    names = []

    def number(name):
        if name not in names:
            names.append(name)
        return names.index(name)

    def copy(name, src, dst, device):
        return pltpu.make_async_remote_copy(
            src_ref=src,
            dst_ref=dst,
            send_sem=ssem.at[number(name)],
            recv_sem=rsem.at[number(name)],
            device_id=device,
            device_id_type=MESH,
        )

    def wait_bytes(sem, name, ref):
        pltpu.make_async_copy(ref, ref, sem.at[number(name)]).wait()

    drains = []

    def send(axis, name, src, dst):
        me = c if axis == "mp" else b
        peers(axis, lambda peer: copy(name, src(peer), dst.at[me], at(axis, peer)).start())
        drains.append(lambda: wait_bytes(ssem, name, dst.at[pl.ds(0, G - 1)]))

    def send_used(name, src, dst):
        def act(peer):
            @pl.when(peer < USED)
            def _():
                copy(name, src(peer), dst.at[b], (peer, c)).start()

        peers("frames", act)

        def drain():
            @pl.when(scans)
            def _():
                wait_bytes(ssem, name, dst.at[pl.ds(0, USED - 1)])

            @pl.when(jnp.logical_not(scans))
            def _():
                wait_bytes(ssem, name, dst.at[pl.ds(0, USED)])

        drains.append(drain)

    def arrived(name, dst):
        wait_bytes(rsem, name, dst.at[pl.ds(0, G - 1)])

    barrier = pltpu.get_barrier_semaphore()
    for axis in ("frames", "mp"):
        peers(
            axis,
            lambda peer, axis=axis: pl.semaphore_signal(
                barrier, inc=1, device_id=at(axis, peer), device_id_type=MESH
            ),
        )

    load("wb0", wbc_hbm.at[0], wb0.at[cy, cx])
    load("dec", dec_hbm, din)
    load("a", a_hbm, araw)
    load("skip", skip_hbm, skip)
    load("out0", wout_hbm.at[0, core], blk0.at[cy, cx, core, :, pl.ds(0, WIDE)])
    load("bc1", wbc_hbm.at[1, core], blk0.at[cy, cx, core, :, pl.ds(WIDE, PAIR)])
    load("out1", wout_hbm.at[1, core], blk1.at[cy, cx, core])

    loads["x"].wait()
    for pair in range(G):
        if pair < USED:
            even = xin[2 * pair].astype(F32)
            odd = xin[2 * pair + 1].astype(F32) if 2 * pair + 1 < JOINTS else jnp.zeros_like(even)
            tmp[0, pl.ds(pair * G, G)] = jnp.concatenate([even, odd], axis=1)
        else:
            tmp[0, pl.ds(pair * G, G)] = jnp.zeros((G, PAIR), F32)
    for frame in range(G):
        send_x[frame] = tmp[0, pl.ds(frame, G, stride=G), :].astype(BF16)
    buf_x[c] = send_x[c]

    pl.semaphore_wait(barrier, 2 * (G - 1))

    send("mp", "x", lambda peer: send_x.at[peer], buf_x)
    loads["wb0"].wait()
    peers("mp", lambda peer: copy("wb0", wb0.at[cy, cx], wb0.at[cy, cx], at("mp", peer)).start())
    flat_wb0 = wb0.reshape(G, 2, HALF // 2, PAIR).at[pl.ds(0, G - 1)]
    drains.append(lambda: wait_bytes(ssem, "wb0", flat_wb0))
    loads["dec"].wait()
    dsend[...] = jnp.concatenate([din[0], din[1]], axis=1)
    send("frames", "dec", lambda peer: dsend, dall)
    dall[b] = dsend[...]
    loads["a"].wait()
    for joint in range(JOINTS):
        for layer in range(LAYERS):
            ain[layer, pl.ds(joint, 1)] = araw[joint, pl.ds(layer, 1)]
    row = lax.broadcasted_iota(jnp.int32, (2 * G, JOINTS), 0)
    pick = (lax.broadcasted_iota(jnp.int32, (2 * G, JOINTS), 1) == 2 * lax.rem(row, G) + row // G).astype(F32)
    for layer in range(LAYERS):
        half = jnp.dot(pick, ain[layer], precision=HI, preferred_element_type=F32)
        aperm[layer] = lax.dot_general(
            half, pick, (((1,), (1,)), ((), ())), precision=HI, preferred_element_type=F32
        )
        buf_c[layer, pl.ds(USED, G - USED)] = jnp.zeros((G - USED, G, PAIR), BF16)
    for name in ("skip", "out0", "bc1", "out1"):
        loads[name].wait()

    blocks = (blk0, blk1)

    def step1(n):
        blk = blocks[n]
        for i in range(1, SIDE):
            to = lax.rem(cy + i * core, SIDE) * SIDE + lax.rem(cx + i * (1 - core), SIDE)
            part = blk.at[cy, cx, core]
            copy(f"one{n}", part, part, (b, to)).start()
        drains.append(lambda: wait_bytes(ssem, f"one{n}", blk.at[0, pl.ds(0, SIDE - 1), 0]))

    def step2(n):
        blk = blocks[n]
        wait_bytes(rsem, f"one{n}", blk.at[0, pl.ds(0, SIDE - 1), 0])

        @pl.when(core == 0)
        def _():
            for i in (1, SIDE - 1):
                part = blk.at[cy, :, 0]
                copy(f"two{n}", part, part, (b, lax.rem(cy + i, SIDE) * SIDE + cx)).start()

        @pl.when(core == 1)
        def _():
            for i in (1, SIDE - 1):
                part = blk.at[:, cx, 1]
                copy(f"two{n}", part, part, (b, cy * SIDE + lax.rem(cx + i, SIDE))).start()

        drains.append(lambda: wait_bytes(ssem, f"two{n}", blk.at[pl.ds(0, 2), :, 0]))

    def step2b(n):
        blk = blocks[n]
        wait_bytes(rsem, f"two{n}", blk.at[pl.ds(0, 2), :, 0])

        @pl.when(core == 0)
        def _():
            for i in (1, SIDE - 1):
                part = blk.at[lax.rem(cy + SIDE - i, SIDE), pl.ds(i // 2 * 2, 2), 0]
                copy(f"far{n}", part, part, (b, lax.rem(cy + i, SIDE) * SIDE + cx)).start()

        @pl.when(core == 1)
        def _():
            for i in (1, SIDE - 1):
                part = blk.at[pl.ds(i // 2 * 2, 2), lax.rem(cx + SIDE - i, SIDE), 1]
                copy(f"far{n}", part, part, (b, cy * SIDE + lax.rem(cx + i, SIDE))).start()

        drains.append(lambda: wait_bytes(ssem, f"far{n}", blk.at[0, :, 0]))

    def step3(n):
        blk = blocks[n]
        wait_bytes(rsem, f"far{n}", blk.at[0, :, 0])
        part = blk.at[:, :, core]
        copy(f"three{n}", part, part, (b + 1 - 2 * core, c)).start()
        drains.append(lambda: wait_bytes(ssem, f"three{n}", blk.at[:, :, 0]))

    def step4(n):
        wait_bytes(rsem, f"three{n}", blocks[n].at[:, :, 0])

    step1(0)
    step1(1)

    def spread(buf, dst):
        for q in range(G // 2):
            even, odd = mix_halves(buf[2 * q].astype(F32), buf[2 * q + 1].astype(F32))
            lanes = pl.ds(q * PAIR, PAIR)
            dst[pl.ds(0, G), lanes] = even.astype(dst.dtype)
            dst[pl.ds(G, G), lanes] = odd.astype(dst.dtype)

    def decay_scales():
        arrived("dec", dall)
        a = dall[...].reshape(FRAMES, PAIR)
        later = lax.broadcasted_iota(jnp.int32, (FRAMES, FRAMES), 0)
        earlier = lax.broadcasted_iota(jnp.int32, (FRAMES, FRAMES), 1)
        logs = jnp.dot(
            (earlier <= later).astype(F32), jnp.log(a), precision=HI, preferred_element_type=F32
        )
        for l in range(LAYERS):
            left = left_half((FRAMES, PAIR))
            mine = left if l == 0 else jnp.logical_not(left)
            la = jnp.where(mine, logs, pltpu.roll(logs, HALF, 1))
            da = 1.0 - jnp.where(mine, a, pltpu.roll(a, HALF, 1))
            for t in range(FRAMES // CHUNK):
                rows = slice(t * CHUNK, (t + 1) * CHUNK)
                rel = la[rows] - la[t * CHUNK + CHUNK // 2 - 1 : t * CHUNK + CHUNK // 2]
                scale_e[l, pl.ds(t * CHUNK, CHUNK)] = jnp.exp(rel)
                scale_w[l, pl.ds(t * CHUNK, CHUNK)] = da[rows] * jnp.exp(-rel)
            end = la[CHUNK - 1 : CHUNK]
            scale_x[l] = da[:CHUNK] * jnp.exp(end - la[:CHUNK])
            scale_f[l] = jnp.exp(la[CHUNK:] - end)

    arrived("x", buf_x)
    spread(buf_x, xs)

    for layer in range(LAYERS):

        def named(name, layer=layer):
            return f"{name}{layer}"

        mixed32 = jnp.dot(aperm[layer], xs[...], precision=HI, preferred_element_type=F32)
        mixed = mixed32.astype(BF16)
        mixed32 = mixed.astype(F32)
        for q in range(G // 2):
            lanes = slice(q * PAIR, (q + 1) * PAIR)
            pieces = mix_halves(mixed32[:G, lanes], mixed32[G:, lanes])
            for i in range(2):
                send_a[layer, 2 * q + i] = pieces[i].astype(BF16)
        send("mp", named("a"), lambda peer: send_a.at[layer, peer], buf_a.at[layer])
        buf_a[layer, c] = send_a[layer, c]
        if layer == 1:
            step2(1)
        if layer == 0:
            wait_bytes(rsem, "wb0", flat_wb0)
            weights = wb0[...].reshape(WIDE, PAIR)
        else:
            weights = blk0[:, :, :, :, pl.ds(WIDE, PAIR)].reshape(WIDE, PAIR)
        coef = jnp.dot(mixed, weights, preferred_element_type=F32)
        in_b, out_c = mix_halves(coef[:G], coef[G:])
        for pair in range(USED):
            send_k[layer, pair, :, pl.ds(0, PAIR)] = in_b[pair : pair + 1]
            send_k[layer, pair, :, pl.ds(PAIR, PAIR)] = out_c[pair : pair + 1]
        send_used(named("k"), lambda peer: send_k.at[layer, peer], buf_k.at[layer])

        if layer == 0:
            step2(0)
        arrived(named("a"), buf_a.at[layer])
        tmp[0] = buf_a[layer].reshape(FRAMES, PAIR).astype(F32)
        for pair in range(USED):
            send_b[layer, pair] = tmp[0, pl.ds(pair, G, stride=G), :].astype(BF16)
        send_used(named("b"), lambda peer: send_b.at[layer, peer], buf_b.at[layer])

        @pl.when(scans)
        def _():
            buf_b[layer, b] = send_b[layer, b]
            buf_k[layer, b] = send_k[layer, b]
            arrived(named("k"), buf_k.at[layer])
            for block in range(G):
                for part in range(2):
                    tmp[1 + part, pl.ds(block, 1)] = buf_k[layer, block, :, pl.ds(part * PAIR, PAIR)]
            for part in range(2):
                send_g[layer, :, pl.ds(part * PAIR, PAIR)] = tmp[1 + part, pl.ds(0, G)].astype(BF16)
            peers(
                "mp",
                lambda peer: copy(
                    named("g"), send_g.at[layer], buf_g.at[layer, c], (b, peer)
                ).start(),
            )
            buf_g[layer, c] = send_g[layer]

        def drain_g(layer=layer):
            @pl.when(scans)
            def _():
                wait_bytes(ssem, f"g{layer}", buf_g.at[layer, pl.ds(0, G - 1)])

        drains.append(drain_g)
        if layer == 0:
            step2b(0)
        if layer == 1:
            step2b(1)
        if layer == 0:
            decay_scales()

        @pl.when(scans)
        def _():
            arrived(named("g"), buf_g.at[layer])
            for part in range(2):
                tmp[1 + part] = buf_g[layer, :, :, pl.ds(part * PAIR, PAIR)].reshape(FRAMES, PAIR).astype(F32)
            bp, cp = [
                jnp.concatenate([tmp[1 + part, pl.ds(k, G, stride=G), :] for k in range(G)], axis=0)
                for part in range(2)
            ]
            bp = bp.astype(BF16)
            left = left_half((FRAMES, PAIR))
            causal = lax.broadcasted_iota(jnp.int32, (CHUNK, CHUNK), 1) <= lax.broadcasted_iota(
                jnp.int32, (CHUNK, CHUNK), 0
            )

            def grid(cj, bj, masked):
                g = lax.dot_general(
                    cj, bj, (((1,), (1,)), ((), ())), preferred_element_type=F32
                )
                g = jnp.where(causal, g, 0.0) if masked else g
                first = g.astype(BF16)
                return jnp.concatenate([first, (g - first.astype(F32)).astype(BF16), first], axis=1)

            grids = []
            for j in range(2):
                cj = jnp.where(left if j == 0 else jnp.logical_not(left), cp, 0.0).astype(BF16)
                grids.append(
                    (
                        grid(cj[:CHUNK], bp[:CHUNK], True),
                        grid(cj[CHUNK:], bp[CHUNK:], True),
                        grid(cj[CHUNK:], bp[:CHUNK], False),
                    )
                )
            arrived(named("b"), buf_b.at[layer])
            m = buf_b[layer].reshape(FRAMES, PAIR).astype(F32)
            v = m * scale_w[layer]
            vx = m[:CHUNK] * scale_x[layer]
            values = []
            for p in (v[:CHUNK], v[CHUNK:], vx):
                first = p.astype(BF16)
                rest = (p - first.astype(F32)).astype(BF16)
                values.append(jnp.concatenate([first, first, rest], axis=0))
            y0, y1, yx = [
                jnp.where(
                    left[:CHUNK],
                    jnp.dot(grids[0][i], values[i], preferred_element_type=F32),
                    jnp.dot(grids[1][i], values[i], preferred_element_type=F32),
                )
                for i in range(3)
            ]
            gain = skip[pl.ds(layer, 1), :]
            gain = jnp.concatenate([gain, gain], axis=1)
            low = y0 * scale_e[layer, pl.ds(0, CHUNK)] + gain * m[:CHUNK]
            high = (
                y1 * scale_e[layer, pl.ds(CHUNK, CHUNK)] + yx * scale_f[layer] + gain * m[CHUNK:]
            )
            send_c[layer, pl.ds(0, G // 2)] = low.astype(BF16).reshape(G // 2, G, PAIR)
            send_c[layer, pl.ds(G // 2, G // 2)] = high.astype(BF16).reshape(G // 2, G, PAIR)
            peers(
                "frames",
                lambda peer: copy(
                    named("c"), send_c.at[layer, peer], buf_c.at[layer, b], (peer, c)
                ).start(),
            )
            buf_c[layer, b] = send_c[layer, b]

        def drain_c(layer=layer):
            @pl.when(scans)
            def _():
                wait_bytes(ssem, f"c{layer}", buf_c.at[layer, pl.ds(0, G - 1)])

        drains.append(drain_c)
        if layer == 0:
            step3(0)
        if layer == 1:
            step3(1)

        @pl.when(scans)
        def _():
            wait_bytes(rsem, named("c"), buf_c.at[layer, pl.ds(0, USED - 1)])

        @pl.when(jnp.logical_not(scans))
        def _():
            wait_bytes(rsem, named("c"), buf_c.at[layer, pl.ds(0, USED)])

        tmp[0] = buf_c[layer].reshape(FRAMES, PAIR).astype(F32)
        for frame in range(G):
            send_d[layer, frame] = tmp[0, pl.ds(frame, G, stride=G), :].astype(BF16)
        send("mp", named("d"), lambda peer: send_d.at[layer, peer], buf_d.at[layer])
        buf_d[layer, c] = send_d[layer, c]

        if layer == 0:
            step4(0)
        if layer == 1:
            step4(1)
        arrived(named("d"), buf_d.at[layer])
        spread(buf_d.at[layer], res)
        weights = blocks[layer][:, :, :, :, pl.ds(0, WIDE)].reshape(WIDE, WIDE)
        xs[...] += jnp.dot(res[...], weights, preferred_element_type=F32)

    for q in range(G // 2):
        lanes = pl.ds(q * PAIR, PAIR)
        pieces = mix_halves(xs[pl.ds(0, G), lanes], xs[pl.ds(G, G), lanes])
        send_e[2 * q] = pieces[0]
        send_e[2 * q + 1] = pieces[1]
    send("mp", "e", lambda peer: send_e.at[peer], buf_e)
    buf_e[c] = send_e[c]
    for drain in drains:
        drain()
    arrived("e", buf_e)
    out_ref[...] = buf_e[...]


def shards(motion, adjacency, w_bc, decay, skip, w_out):
    vm = pltpu.VMEM
    part = HALF // 2
    out = pl.pallas_call(
        body,
        out_shape=jax.ShapeDtypeStruct((G, G, PAIR), F32),
        in_specs=[pl.BlockSpec(memory_space=pltpu.HBM)] * 6,
        out_specs=pl.BlockSpec(memory_space=vm),
        scratch_shapes=[
            vm((JOINTS, G, HALF), BF16),
            vm((JOINTS, LAYERS, JOINTS), F32),
            vm((LAYERS, JOINTS, JOINTS), F32),
            vm((LAYERS, G, HALF), F32),
            vm((LAYERS, HALF), F32),
            vm((SIDE, SIDE, 2, part, PAIR), BF16),
            vm((SIDE, SIDE, 2, part, WIDE + PAIR), BF16),
            vm((SIDE, SIDE, 2, part, WIDE), BF16),
            vm((G, PAIR), F32),
            vm((G, G, PAIR), F32),
            vm((LAYERS, FRAMES, PAIR), F32),
            vm((LAYERS, FRAMES, PAIR), F32),
            vm((LAYERS, CHUNK, PAIR), F32),
            vm((LAYERS, CHUNK, PAIR), F32),
            vm((LAYERS, 2 * G, 2 * G), F32),
            vm((G, G, PAIR), BF16),
            vm((G, G, PAIR), BF16),
            vm((LAYERS, G, G, PAIR), BF16),
            vm((LAYERS, G, G, PAIR), BF16),
            vm((LAYERS, USED, 1, 2 * PAIR), F32),
            vm((LAYERS, G, 1, 2 * PAIR), F32),
            vm((LAYERS, G, 2 * PAIR), BF16),
            vm((LAYERS, G, G, 2 * PAIR), BF16),
            vm((LAYERS, USED, G, PAIR), BF16),
            vm((LAYERS, G, G, PAIR), BF16),
            vm((LAYERS, G, G, PAIR), BF16),
            vm((LAYERS, G, G, PAIR), BF16),
            vm((LAYERS, G, G, PAIR), BF16),
            vm((LAYERS, G, G, PAIR), BF16),
            vm((G, G, PAIR), F32),
            vm((G, G, PAIR), F32),
            vm((3, FRAMES, PAIR), F32),
            vm((2 * G, WIDE), F32),
            vm((2 * G, WIDE), BF16),
            pltpu.SemaphoreType.DMA((8,)),
            pltpu.SemaphoreType.DMA((24,)),
            pltpu.SemaphoreType.DMA((24,)),
        ],
        compiler_params=pltpu.CompilerParams(
            collective_id=0, has_side_effects=True, vmem_limit_bytes=56 * 2**20
        ),
    )(
        motion.transpose(1, 0, 2),
        adjacency.transpose(1, 0, 2),
        w_bc.reshape(LAYERS, 2, part, PAIR),
        decay,
        skip,
        w_out.reshape(LAYERS, 2, part, WIDE),
    )
    return out.reshape(G, 2 * G, HALF)[:, :JOINTS]


def solution(mesh):
    return jax.shard_map(
        shards,
        mesh=mesh,
        in_specs=(
            P("frames", None, "mp"),
            P(),
            P(None, "mp", None),
            P(None, "frames", "mp"),
            P(None, "mp"),
            P(None, "mp", None),
        ),
        out_specs=P("frames", None, "mp"),
        check_vma=False,
    )
```

```python
import jax
import jax.numpy as jnp
from jax import lax
from jax.experimental import pallas as pl
from jax.experimental.pallas import tpu as pltpu
from jax.sharding import PartitionSpec as P

MESH = pl.DeviceIdType.MESH
HI = lax.Precision.HIGHEST
F32, BF16 = jnp.float32, jnp.bfloat16
LAYERS = 2
JOINTS = 25
G = 16
SIDE = 4
USED = 13
HALF, PAIR = 64, 128
WIDE = G * HALF
FRAMES = 256
CHUNK = 128


def left_half(shape):
    return lax.broadcasted_iota(jnp.int32, shape, len(shape) - 1) % PAIR < HALF


def mix_halves(first, second):
    left = left_half(first.shape)
    return (
        jnp.where(left, first, pltpu.roll(second, HALF, 1)),
        jnp.where(left, pltpu.roll(first, HALF, 1), second),
    )


def body(
    x_hbm, a_hbm, wbc_hbm, dec_hbm, skip_hbm, wout_hbm, out_ref,
    xin, araw, ain, din, skip, wb0, blk0, blk1, dsend, dall,
    scale_e, scale_w, scale_x, scale_f, aperm,
    send_x, buf_x, send_a, buf_a, send_k, buf_k, send_g, buf_g,
    send_b, buf_b, send_c, buf_c, send_d, buf_d, send_e, buf_e,
    tmp, xs, res, lsem, ssem, rsem,
):
    b, c = lax.axis_index("frames"), lax.axis_index("mp")
    core = lax.rem(b, 2)
    cy, cx = c // SIDE, lax.rem(c, SIDE)
    scans = b < USED

    loads = {}

    def load(name, src, dst):
        loads[name] = pltpu.make_async_copy(src, dst, lsem.at[len(loads)])
        loads[name].start()

    load("x", x_hbm, xin)

    def at(axis, peer):
        return (b, peer) if axis == "mp" else (peer, c)

    def peers(axis, act):
        def off(k, half):
            return half + (k + 1) // 2 * (1 - 2 * lax.rem(k + 1, 2))

        def one(k, carry):
            if axis == "mp":
                to_y = lax.rem(cy + off(k // SIDE, SIDE // 2), SIDE)
                to_x = lax.rem(cx + off(lax.rem(k, SIDE), SIDE // 2), SIDE)
                act(to_y * SIDE + to_x)
            else:
                act(lax.rem(b + off(k, G // 2), G))
            return carry

        lax.fori_loop(0, G - 1, one, 0, unroll=3)

    names = []

    def number(name):
        if name not in names:
            names.append(name)
        return names.index(name)

    def copy(name, src, dst, device):
        return pltpu.make_async_remote_copy(
            src_ref=src,
            dst_ref=dst,
            send_sem=ssem.at[number(name)],
            recv_sem=rsem.at[number(name)],
            device_id=device,
            device_id_type=MESH,
        )

    def wait_bytes(sem, name, ref):
        pltpu.make_async_copy(ref, ref, sem.at[number(name)]).wait()

    drains = []

    def send(axis, name, src, dst):
        me = c if axis == "mp" else b
        peers(axis, lambda peer: copy(name, src(peer), dst.at[me], at(axis, peer)).start())
        drains.append(lambda: wait_bytes(ssem, name, dst.at[pl.ds(0, G - 1)]))

    def send_used(name, src, dst):
        def act(peer):
            @pl.when(peer < USED)
            def _():
                copy(name, src(peer), dst.at[b], (peer, c)).start()

        peers("frames", act)

        def drain():
            @pl.when(scans)
            def _():
                wait_bytes(ssem, name, dst.at[pl.ds(0, USED - 1)])

            @pl.when(jnp.logical_not(scans))
            def _():
                wait_bytes(ssem, name, dst.at[pl.ds(0, USED)])

        drains.append(drain)

    def arrived(name, dst):
        wait_bytes(rsem, name, dst.at[pl.ds(0, G - 1)])

    barrier = pltpu.get_barrier_semaphore()
    for axis in ("frames", "mp"):
        peers(
            axis,
            lambda peer, axis=axis: pl.semaphore_signal(
                barrier, inc=1, device_id=at(axis, peer), device_id_type=MESH
            ),
        )

    load("wb0", wbc_hbm.at[0], wb0.at[cy, cx])
    load("dec", dec_hbm, din)
    load("a", a_hbm, araw)
    load("skip", skip_hbm, skip)
    load("out0", wout_hbm.at[0, core], blk0.at[cy, cx, core, :, pl.ds(0, WIDE)])
    load("bc1", wbc_hbm.at[1, core], blk0.at[cy, cx, core, :, pl.ds(WIDE, PAIR)])
    load("out1", wout_hbm.at[1, core], blk1.at[cy, cx, core])

    loads["x"].wait()
    for pair in range(G):
        if pair < USED:
            even = xin[2 * pair].astype(F32)
            odd = xin[2 * pair + 1].astype(F32) if 2 * pair + 1 < JOINTS else jnp.zeros_like(even)
            tmp[0, pl.ds(pair * G, G)] = jnp.concatenate([even, odd], axis=1)
        else:
            tmp[0, pl.ds(pair * G, G)] = jnp.zeros((G, PAIR), F32)
    for frame in range(G):
        send_x[frame] = tmp[0, pl.ds(frame, G, stride=G), :].astype(BF16)
    buf_x[c] = send_x[c]

    pl.semaphore_wait(barrier, 2 * (G - 1))

    send("mp", "x", lambda peer: send_x.at[peer], buf_x)
    loads["wb0"].wait()
    peers("mp", lambda peer: copy("wb0", wb0.at[cy, cx], wb0.at[cy, cx], at("mp", peer)).start())
    flat_wb0 = wb0.reshape(G, 2, HALF // 2, PAIR).at[pl.ds(0, G - 1)]
    drains.append(lambda: wait_bytes(ssem, "wb0", flat_wb0))
    loads["dec"].wait()
    dsend[...] = jnp.concatenate([din[0], din[1]], axis=1)
    send("frames", "dec", lambda peer: dsend, dall)
    dall[b] = dsend[...]
    loads["a"].wait()
    for joint in range(JOINTS):
        for layer in range(LAYERS):
            ain[layer, pl.ds(joint, 1)] = araw[joint, pl.ds(layer, 1)]
    row = lax.broadcasted_iota(jnp.int32, (2 * G, JOINTS), 0)
    pick = (lax.broadcasted_iota(jnp.int32, (2 * G, JOINTS), 1) == 2 * lax.rem(row, G) + row // G).astype(F32)
    for layer in range(LAYERS):
        half = jnp.dot(pick, ain[layer], precision=HI, preferred_element_type=F32)
        aperm[layer] = lax.dot_general(
            half, pick, (((1,), (1,)), ((), ())), precision=HI, preferred_element_type=F32
        )
        buf_c[layer, pl.ds(USED, G - USED)] = jnp.zeros((G - USED, G, PAIR), BF16)
    for name in ("skip", "out0", "bc1", "out1"):
        loads[name].wait()

    blocks = (blk0, blk1)

    def step1(n):
        blk = blocks[n]
        for i in range(1, SIDE):
            to = lax.rem(cy + i * core, SIDE) * SIDE + lax.rem(cx + i * (1 - core), SIDE)
            part = blk.at[cy, cx, core]
            copy(f"one{n}", part, part, (b, to)).start()
        drains.append(lambda: wait_bytes(ssem, f"one{n}", blk.at[0, pl.ds(0, SIDE - 1), 0]))

    def step2(n):
        blk = blocks[n]
        wait_bytes(rsem, f"one{n}", blk.at[0, pl.ds(0, SIDE - 1), 0])

        @pl.when(core == 0)
        def _():
            for i in (1, SIDE - 1):
                part = blk.at[cy, :, 0]
                copy(f"two{n}", part, part, (b, lax.rem(cy + i, SIDE) * SIDE + cx)).start()

        @pl.when(core == 1)
        def _():
            for i in (1, SIDE - 1):
                part = blk.at[:, cx, 1]
                copy(f"two{n}", part, part, (b, cy * SIDE + lax.rem(cx + i, SIDE))).start()

        drains.append(lambda: wait_bytes(ssem, f"two{n}", blk.at[pl.ds(0, 2), :, 0]))

    def step2b(n):
        blk = blocks[n]
        wait_bytes(rsem, f"two{n}", blk.at[pl.ds(0, 2), :, 0])

        @pl.when(core == 0)
        def _():
            for i in (1, SIDE - 1):
                part = blk.at[lax.rem(cy + SIDE - i, SIDE), pl.ds(i // 2 * 2, 2), 0]
                copy(f"far{n}", part, part, (b, lax.rem(cy + i, SIDE) * SIDE + cx)).start()

        @pl.when(core == 1)
        def _():
            for i in (1, SIDE - 1):
                part = blk.at[pl.ds(i // 2 * 2, 2), lax.rem(cx + SIDE - i, SIDE), 1]
                copy(f"far{n}", part, part, (b, cy * SIDE + lax.rem(cx + i, SIDE))).start()

        drains.append(lambda: wait_bytes(ssem, f"far{n}", blk.at[0, :, 0]))

    def step3(n):
        blk = blocks[n]
        wait_bytes(rsem, f"far{n}", blk.at[0, :, 0])
        part = blk.at[:, :, core]
        copy(f"three{n}", part, part, (b + 1 - 2 * core, c)).start()
        drains.append(lambda: wait_bytes(ssem, f"three{n}", blk.at[:, :, 0]))

    def step4(n):
        wait_bytes(rsem, f"three{n}", blocks[n].at[:, :, 0])


    def spread(buf, dst):
        for q in range(G // 2):
            even, odd = mix_halves(buf[2 * q].astype(F32), buf[2 * q + 1].astype(F32))
            lanes = pl.ds(q * PAIR, PAIR)
            dst[pl.ds(0, G), lanes] = even.astype(dst.dtype)
            dst[pl.ds(G, G), lanes] = odd.astype(dst.dtype)

    def decay_scales():
        arrived("dec", dall)
        a = dall[...].reshape(FRAMES, PAIR)
        later = lax.broadcasted_iota(jnp.int32, (FRAMES, FRAMES), 0)
        earlier = lax.broadcasted_iota(jnp.int32, (FRAMES, FRAMES), 1)
        logs = jnp.dot(
            (earlier <= later).astype(F32), jnp.log(a), precision=HI, preferred_element_type=F32
        )
        for l in range(LAYERS):
            left = left_half((FRAMES, PAIR))
            mine = left if l == 0 else jnp.logical_not(left)
            la = jnp.where(mine, logs, pltpu.roll(logs, HALF, 1))
            da = 1.0 - jnp.where(mine, a, pltpu.roll(a, HALF, 1))
            for t in range(FRAMES // CHUNK):
                rows = slice(t * CHUNK, (t + 1) * CHUNK)
                rel = la[rows] - la[t * CHUNK + CHUNK // 2 - 1 : t * CHUNK + CHUNK // 2]
                scale_e[l, pl.ds(t * CHUNK, CHUNK)] = jnp.exp(rel)
                scale_w[l, pl.ds(t * CHUNK, CHUNK)] = da[rows] * jnp.exp(-rel)
            end = la[CHUNK - 1 : CHUNK]
            scale_x[l] = da[:CHUNK] * jnp.exp(end - la[:CHUNK])
            scale_f[l] = jnp.exp(la[CHUNK:] - end)

    arrived("x", buf_x)
    spread(buf_x, xs)

    for layer in range(LAYERS):

        def named(name, layer=layer):
            return f"{name}{layer}"

        mixed32 = jnp.dot(aperm[layer], xs[...], precision=HI, preferred_element_type=F32)
        mixed = mixed32.astype(BF16)
        mixed32 = mixed.astype(F32)
        for q in range(G // 2):
            lanes = slice(q * PAIR, (q + 1) * PAIR)
            pieces = mix_halves(mixed32[:G, lanes], mixed32[G:, lanes])
            for i in range(2):
                send_a[layer, 2 * q + i] = pieces[i].astype(BF16)
        send("mp", named("a"), lambda peer: send_a.at[layer, peer], buf_a.at[layer])
        buf_a[layer, c] = send_a[layer, c]
        if layer == 1:
            step2(1)
        if layer == 0:
            wait_bytes(rsem, "wb0", flat_wb0)
            weights = wb0[...].reshape(WIDE, PAIR)
        else:
            weights = blk0[:, :, :, :, pl.ds(WIDE, PAIR)].reshape(WIDE, PAIR)
        coef = jnp.dot(mixed, weights, preferred_element_type=F32)
        in_b, out_c = mix_halves(coef[:G], coef[G:])
        for pair in range(USED):
            send_k[layer, pair, :, pl.ds(0, PAIR)] = in_b[pair : pair + 1]
            send_k[layer, pair, :, pl.ds(PAIR, PAIR)] = out_c[pair : pair + 1]
        send_used(named("k"), lambda peer: send_k.at[layer, peer], buf_k.at[layer])

        if layer == 0:
            step1(0)
            step1(1)
        arrived(named("a"), buf_a.at[layer])
        tmp[0] = buf_a[layer].reshape(FRAMES, PAIR).astype(F32)
        for pair in range(USED):
            send_b[layer, pair] = tmp[0, pl.ds(pair, G, stride=G), :].astype(BF16)
        send_used(named("b"), lambda peer: send_b.at[layer, peer], buf_b.at[layer])

        @pl.when(scans)
        def _():
            buf_b[layer, b] = send_b[layer, b]
            buf_k[layer, b] = send_k[layer, b]
            arrived(named("k"), buf_k.at[layer])
            for block in range(G):
                for part in range(2):
                    tmp[1 + part, pl.ds(block, 1)] = buf_k[layer, block, :, pl.ds(part * PAIR, PAIR)]
            for part in range(2):
                send_g[layer, :, pl.ds(part * PAIR, PAIR)] = tmp[1 + part, pl.ds(0, G)].astype(BF16)
            peers(
                "mp",
                lambda peer: copy(
                    named("g"), send_g.at[layer], buf_g.at[layer, c], (b, peer)
                ).start(),
            )
            buf_g[layer, c] = send_g[layer]

        def drain_g(layer=layer):
            @pl.when(scans)
            def _():
                wait_bytes(ssem, f"g{layer}", buf_g.at[layer, pl.ds(0, G - 1)])

        drains.append(drain_g)
        if layer == 0:
            step2(0)
        if layer == 1:
            step2b(1)
        if layer == 0:
            decay_scales()

        @pl.when(scans)
        def _():
            arrived(named("g"), buf_g.at[layer])
            for part in range(2):
                tmp[1 + part] = buf_g[layer, :, :, pl.ds(part * PAIR, PAIR)].reshape(FRAMES, PAIR).astype(F32)
            bp, cp = [
                jnp.concatenate([tmp[1 + part, pl.ds(k, G, stride=G), :] for k in range(G)], axis=0)
                for part in range(2)
            ]
            bp = bp.astype(BF16)
            left = left_half((FRAMES, PAIR))
            causal = lax.broadcasted_iota(jnp.int32, (CHUNK, CHUNK), 1) <= lax.broadcasted_iota(
                jnp.int32, (CHUNK, CHUNK), 0
            )

            def grid(cj, bj, masked):
                g = lax.dot_general(
                    cj, bj, (((1,), (1,)), ((), ())), preferred_element_type=F32
                )
                g = jnp.where(causal, g, 0.0) if masked else g
                first = g.astype(BF16)
                return jnp.concatenate([first, (g - first.astype(F32)).astype(BF16), first], axis=1)

            grids = []
            for j in range(2):
                cj = jnp.where(left if j == 0 else jnp.logical_not(left), cp, 0.0).astype(BF16)
                grids.append(
                    (
                        grid(cj[:CHUNK], bp[:CHUNK], True),
                        grid(cj[CHUNK:], bp[CHUNK:], True),
                        grid(cj[CHUNK:], bp[:CHUNK], False),
                    )
                )
            arrived(named("b"), buf_b.at[layer])
            m = buf_b[layer].reshape(FRAMES, PAIR).astype(F32)
            v = m * scale_w[layer]
            vx = m[:CHUNK] * scale_x[layer]
            values = []
            for p in (v[:CHUNK], v[CHUNK:], vx):
                first = p.astype(BF16)
                rest = (p - first.astype(F32)).astype(BF16)
                values.append(jnp.concatenate([first, first, rest], axis=0))
            y0, y1, yx = [
                jnp.where(
                    left[:CHUNK],
                    jnp.dot(grids[0][i], values[i], preferred_element_type=F32),
                    jnp.dot(grids[1][i], values[i], preferred_element_type=F32),
                )
                for i in range(3)
            ]
            gain = skip[pl.ds(layer, 1), :]
            gain = jnp.concatenate([gain, gain], axis=1)
            low = y0 * scale_e[layer, pl.ds(0, CHUNK)] + gain * m[:CHUNK]
            high = (
                y1 * scale_e[layer, pl.ds(CHUNK, CHUNK)] + yx * scale_f[layer] + gain * m[CHUNK:]
            )
            send_c[layer, pl.ds(0, G // 2)] = low.astype(BF16).reshape(G // 2, G, PAIR)
            send_c[layer, pl.ds(G // 2, G // 2)] = high.astype(BF16).reshape(G // 2, G, PAIR)
            peers(
                "frames",
                lambda peer: copy(
                    named("c"), send_c.at[layer, peer], buf_c.at[layer, b], (peer, c)
                ).start(),
            )
            buf_c[layer, b] = send_c[layer, b]

        def drain_c(layer=layer):
            @pl.when(scans)
            def _():
                wait_bytes(ssem, f"c{layer}", buf_c.at[layer, pl.ds(0, G - 1)])

        drains.append(drain_c)
        if layer == 0:
            step2b(0)
        if layer == 1:
            step3(1)

        @pl.when(scans)
        def _():
            wait_bytes(rsem, named("c"), buf_c.at[layer, pl.ds(0, USED - 1)])

        @pl.when(jnp.logical_not(scans))
        def _():
            wait_bytes(rsem, named("c"), buf_c.at[layer, pl.ds(0, USED)])

        tmp[0] = buf_c[layer].reshape(FRAMES, PAIR).astype(F32)
        for frame in range(G):
            send_d[layer, frame] = tmp[0, pl.ds(frame, G, stride=G), :].astype(BF16)
        send("mp", named("d"), lambda peer: send_d.at[layer, peer], buf_d.at[layer])
        buf_d[layer, c] = send_d[layer, c]

        if layer == 0:
            step3(0)
            step4(0)
        if layer == 1:
            step4(1)
        arrived(named("d"), buf_d.at[layer])
        spread(buf_d.at[layer], res)
        weights = blocks[layer][:, :, :, :, pl.ds(0, WIDE)].reshape(WIDE, WIDE)
        xs[...] += jnp.dot(res[...], weights, preferred_element_type=F32)

    for q in range(G // 2):
        lanes = pl.ds(q * PAIR, PAIR)
        pieces = mix_halves(xs[pl.ds(0, G), lanes], xs[pl.ds(G, G), lanes])
        send_e[2 * q] = pieces[0]
        send_e[2 * q + 1] = pieces[1]
    send("mp", "e", lambda peer: send_e.at[peer], out_ref)
    out_ref[c] = send_e[c]
    for drain in drains:
        drain()
    arrived("e", out_ref)


def shards(motion, adjacency, w_bc, decay, skip, w_out):
    vm = pltpu.VMEM
    part = HALF // 2
    out = pl.pallas_call(
        body,
        out_shape=jax.ShapeDtypeStruct((G, G, PAIR), F32),
        in_specs=[pl.BlockSpec(memory_space=pltpu.HBM)] * 6,
        out_specs=pl.BlockSpec(memory_space=vm),
        scratch_shapes=[
            vm((JOINTS, G, HALF), BF16),
            vm((JOINTS, LAYERS, JOINTS), F32),
            vm((LAYERS, JOINTS, JOINTS), F32),
            vm((LAYERS, G, HALF), F32),
            vm((LAYERS, HALF), F32),
            vm((SIDE, SIDE, 2, part, PAIR), BF16),
            vm((SIDE, SIDE, 2, part, WIDE + PAIR), BF16),
            vm((SIDE, SIDE, 2, part, WIDE), BF16),
            vm((G, PAIR), F32),
            vm((G, G, PAIR), F32),
            vm((LAYERS, FRAMES, PAIR), F32),
            vm((LAYERS, FRAMES, PAIR), F32),
            vm((LAYERS, CHUNK, PAIR), F32),
            vm((LAYERS, CHUNK, PAIR), F32),
            vm((LAYERS, 2 * G, 2 * G), F32),
            vm((G, G, PAIR), BF16),
            vm((G, G, PAIR), BF16),
            vm((LAYERS, G, G, PAIR), BF16),
            vm((LAYERS, G, G, PAIR), BF16),
            vm((LAYERS, USED, 1, 2 * PAIR), F32),
            vm((LAYERS, G, 1, 2 * PAIR), F32),
            vm((LAYERS, G, 2 * PAIR), BF16),
            vm((LAYERS, G, G, 2 * PAIR), BF16),
            vm((LAYERS, USED, G, PAIR), BF16),
            vm((LAYERS, G, G, PAIR), BF16),
            vm((LAYERS, G, G, PAIR), BF16),
            vm((LAYERS, G, G, PAIR), BF16),
            vm((LAYERS, G, G, PAIR), BF16),
            vm((LAYERS, G, G, PAIR), BF16),
            vm((G, G, PAIR), F32),
            vm((G, G, PAIR), F32),
            vm((3, FRAMES, PAIR), F32),
            vm((2 * G, WIDE), F32),
            vm((2 * G, WIDE), BF16),
            pltpu.SemaphoreType.DMA((8,)),
            pltpu.SemaphoreType.DMA((24,)),
            pltpu.SemaphoreType.DMA((24,)),
        ],
        compiler_params=pltpu.CompilerParams(
            collective_id=0, has_side_effects=True, vmem_limit_bytes=56 * 2**20
        ),
    )(
        motion.transpose(1, 0, 2),
        adjacency.transpose(1, 0, 2),
        w_bc.reshape(LAYERS, 2, part, PAIR),
        decay,
        skip,
        w_out.reshape(LAYERS, 2, part, WIDE),
    )
    return out.reshape(G, 2 * G, HALF)[:, :JOINTS]


def solution(mesh):
    return jax.shard_map(
        shards,
        mesh=mesh,
        in_specs=(
            P("frames", None, "mp"),
            P(),
            P(None, "mp", None),
            P(None, "frames", "mp"),
            P(None, "mp"),
            P(None, "mp", None),
        ),
        out_specs=P("frames", None, "mp"),
        check_vma=False,
    )
```

```python
import jax
import jax.numpy as jnp
from jax import lax
from jax.experimental import pallas as pl
from jax.experimental.pallas import tpu as pltpu
from jax.sharding import PartitionSpec as P

MESH = pl.DeviceIdType.MESH
HI = lax.Precision.HIGHEST
F32, BF16 = jnp.float32, jnp.bfloat16
LAYERS = 2
JOINTS = 25
G = 16
SIDE = 4
USED = 13
HALF, PAIR = 64, 128
WIDE = G * HALF
FRAMES = 256
CHUNK = 128


def left_half(shape):
    return lax.broadcasted_iota(jnp.int32, shape, len(shape) - 1) % PAIR < HALF


def mix_halves(first, second):
    left = left_half(first.shape)
    return (
        jnp.where(left, first, pltpu.roll(second, HALF, 1)),
        jnp.where(left, pltpu.roll(first, HALF, 1), second),
    )


def body(
    x_hbm, a_hbm, wbc_hbm, dec_hbm, skip_hbm, wout_hbm, out_ref,
    xin, araw, ain, din, skip, wb0, blk0, blk1, dsend, dall,
    scale_e, scale_w, scale_x, scale_f, aperm,
    send_x, buf_x, send_a, buf_a, send_k, buf_k, send_g, buf_g,
    send_b, buf_b, send_c, buf_c, send_d, buf_d, send_e, buf_e,
    tmp, xs, res, lsem, ssem, rsem,
):
    b, c = lax.axis_index("frames"), lax.axis_index("mp")
    core = lax.rem(b, 2)
    cy, cx = c // SIDE, lax.rem(c, SIDE)
    scans = b < USED

    loads = {}

    def load(name, src, dst):
        loads[name] = pltpu.make_async_copy(src, dst, lsem.at[len(loads)])
        loads[name].start()

    load("x", x_hbm, xin)

    def at(axis, peer):
        return (b, peer) if axis == "mp" else (peer, c)

    def peers(axis, act):
        def off(k, half):
            return half + (k + 1) // 2 * (1 - 2 * lax.rem(k + 1, 2))

        def one(k, carry):
            if axis == "mp":
                to_y = lax.rem(cy + off(k // SIDE, SIDE // 2), SIDE)
                to_x = lax.rem(cx + off(lax.rem(k, SIDE), SIDE // 2), SIDE)
                act(to_y * SIDE + to_x)
            else:
                act(lax.rem(b + off(k, G // 2), G))
            return carry

        lax.fori_loop(0, G - 1, one, 0)

    names = []

    def number(name):
        if name not in names:
            names.append(name)
        return names.index(name)

    def copy(name, src, dst, device):
        return pltpu.make_async_remote_copy(
            src_ref=src,
            dst_ref=dst,
            send_sem=ssem.at[number(name)],
            recv_sem=rsem.at[number(name)],
            device_id=device,
            device_id_type=MESH,
        )

    def wait_bytes(sem, name, ref):
        pltpu.make_async_copy(ref, ref, sem.at[number(name)]).wait()

    drains = []

    def send(axis, name, src, dst):
        me = c if axis == "mp" else b
        peers(axis, lambda peer: copy(name, src(peer), dst.at[me], at(axis, peer)).start())
        drains.append(lambda: wait_bytes(ssem, name, dst.at[pl.ds(0, G - 1)]))

    def send_used(name, src, dst):
        def act(peer):
            @pl.when(peer < USED)
            def _():
                copy(name, src(peer), dst.at[b], (peer, c)).start()

        peers("frames", act)

        def drain():
            @pl.when(scans)
            def _():
                wait_bytes(ssem, name, dst.at[pl.ds(0, USED - 1)])

            @pl.when(jnp.logical_not(scans))
            def _():
                wait_bytes(ssem, name, dst.at[pl.ds(0, USED)])

        drains.append(drain)

    def arrived(name, dst):
        wait_bytes(rsem, name, dst.at[pl.ds(0, G - 1)])

    barrier = pltpu.get_barrier_semaphore()
    for axis in ("frames", "mp"):
        peers(
            axis,
            lambda peer, axis=axis: pl.semaphore_signal(
                barrier, inc=1, device_id=at(axis, peer), device_id_type=MESH
            ),
        )

    load("wb0", wbc_hbm.at[0], wb0.at[cy, cx])
    load("dec", dec_hbm, din)
    load("a", a_hbm, araw)
    load("skip", skip_hbm, skip)
    load("out0", wout_hbm.at[0, core], blk0.at[cy, cx, core, :, pl.ds(0, WIDE)])
    load("bc1", wbc_hbm.at[1, core], blk0.at[cy, cx, core, :, pl.ds(WIDE, PAIR)])
    load("out1", wout_hbm.at[1, core], blk1.at[cy, cx, core])

    loads["x"].wait()
    for pair in range(G):
        if pair < USED:
            even = xin[2 * pair].astype(F32)
            odd = xin[2 * pair + 1].astype(F32) if 2 * pair + 1 < JOINTS else jnp.zeros_like(even)
            tmp[0, pl.ds(pair * G, G)] = jnp.concatenate([even, odd], axis=1)
        else:
            tmp[0, pl.ds(pair * G, G)] = jnp.zeros((G, PAIR), F32)
    for frame in range(G):
        send_x[frame] = tmp[0, pl.ds(frame, G, stride=G), :].astype(BF16)
    buf_x[c] = send_x[c]

    pl.semaphore_wait(barrier, 2 * (G - 1))

    send("mp", "x", lambda peer: send_x.at[peer], buf_x)
    loads["wb0"].wait()
    peers("mp", lambda peer: copy("wb0", wb0.at[cy, cx], wb0.at[cy, cx], at("mp", peer)).start())
    flat_wb0 = wb0.reshape(G, 2, HALF // 2, PAIR).at[pl.ds(0, G - 1)]
    drains.append(lambda: wait_bytes(ssem, "wb0", flat_wb0))
    loads["dec"].wait()
    dsend[...] = jnp.concatenate([din[0], din[1]], axis=1)
    send("frames", "dec", lambda peer: dsend, dall)
    dall[b] = dsend[...]
    loads["a"].wait()
    for joint in range(JOINTS):
        for layer in range(LAYERS):
            ain[layer, pl.ds(joint, 1)] = araw[joint, pl.ds(layer, 1)]
    row = lax.broadcasted_iota(jnp.int32, (2 * G, JOINTS), 0)
    pick = (lax.broadcasted_iota(jnp.int32, (2 * G, JOINTS), 1) == 2 * lax.rem(row, G) + row // G).astype(F32)
    for layer in range(LAYERS):
        half = jnp.dot(pick, ain[layer], precision=HI, preferred_element_type=F32)
        aperm[layer] = lax.dot_general(
            half, pick, (((1,), (1,)), ((), ())), precision=HI, preferred_element_type=F32
        )
        buf_c[layer, pl.ds(USED, G - USED)] = jnp.zeros((G - USED, G, PAIR), BF16)
    for name in ("skip", "out0", "bc1", "out1"):
        loads[name].wait()

    blocks = (blk0, blk1)

    def step1(n):
        blk = blocks[n]
        for i in range(1, SIDE):
            to = lax.rem(cy + i * core, SIDE) * SIDE + lax.rem(cx + i * (1 - core), SIDE)
            part = blk.at[cy, cx, core]
            copy(f"one{n}", part, part, (b, to)).start()
        drains.append(lambda: wait_bytes(ssem, f"one{n}", blk.at[0, pl.ds(0, SIDE - 1), 0]))

    def step2(n):
        blk = blocks[n]
        wait_bytes(rsem, f"one{n}", blk.at[0, pl.ds(0, SIDE - 1), 0])

        @pl.when(core == 0)
        def _():
            for i in (1, SIDE - 1):
                part = blk.at[cy, :, 0]
                copy(f"two{n}", part, part, (b, lax.rem(cy + i, SIDE) * SIDE + cx)).start()

        @pl.when(core == 1)
        def _():
            for i in (1, SIDE - 1):
                part = blk.at[:, cx, 1]
                copy(f"two{n}", part, part, (b, cy * SIDE + lax.rem(cx + i, SIDE))).start()

        drains.append(lambda: wait_bytes(ssem, f"two{n}", blk.at[pl.ds(0, 2), :, 0]))

    def step2b(n):
        blk = blocks[n]
        wait_bytes(rsem, f"two{n}", blk.at[pl.ds(0, 2), :, 0])

        @pl.when(core == 0)
        def _():
            for i in (1, SIDE - 1):
                part = blk.at[lax.rem(cy + SIDE - i, SIDE), pl.ds(i // 2 * 2, 2), 0]
                copy(f"far{n}", part, part, (b, lax.rem(cy + i, SIDE) * SIDE + cx)).start()

        @pl.when(core == 1)
        def _():
            for i in (1, SIDE - 1):
                part = blk.at[pl.ds(i // 2 * 2, 2), lax.rem(cx + SIDE - i, SIDE), 1]
                copy(f"far{n}", part, part, (b, cy * SIDE + lax.rem(cx + i, SIDE))).start()

        drains.append(lambda: wait_bytes(ssem, f"far{n}", blk.at[0, :, 0]))

    def step3(n):
        blk = blocks[n]
        wait_bytes(rsem, f"far{n}", blk.at[0, :, 0])
        part = blk.at[:, :, core]
        copy(f"three{n}", part, part, (b + 1 - 2 * core, c)).start()
        drains.append(lambda: wait_bytes(ssem, f"three{n}", blk.at[:, :, 0]))

    def step4(n):
        wait_bytes(rsem, f"three{n}", blocks[n].at[:, :, 0])


    def spread(buf, dst):
        for q in range(G // 2):
            even, odd = mix_halves(buf[2 * q].astype(F32), buf[2 * q + 1].astype(F32))
            lanes = pl.ds(q * PAIR, PAIR)
            dst[pl.ds(0, G), lanes] = even.astype(dst.dtype)
            dst[pl.ds(G, G), lanes] = odd.astype(dst.dtype)

    def decay_scales():
        arrived("dec", dall)
        a = dall[...].reshape(FRAMES, PAIR)
        later = lax.broadcasted_iota(jnp.int32, (FRAMES, FRAMES), 0)
        earlier = lax.broadcasted_iota(jnp.int32, (FRAMES, FRAMES), 1)
        logs = jnp.dot(
            (earlier <= later).astype(F32), jnp.log(a), precision=HI, preferred_element_type=F32
        )
        for l in range(LAYERS):
            left = left_half((FRAMES, PAIR))
            mine = left if l == 0 else jnp.logical_not(left)
            la = jnp.where(mine, logs, pltpu.roll(logs, HALF, 1))
            da = 1.0 - jnp.where(mine, a, pltpu.roll(a, HALF, 1))
            for t in range(FRAMES // CHUNK):
                rows = slice(t * CHUNK, (t + 1) * CHUNK)
                rel = la[rows] - la[t * CHUNK + CHUNK // 2 - 1 : t * CHUNK + CHUNK // 2]
                scale_e[l, pl.ds(t * CHUNK, CHUNK)] = jnp.exp(rel)
                scale_w[l, pl.ds(t * CHUNK, CHUNK)] = da[rows] * jnp.exp(-rel)
            end = la[CHUNK - 1 : CHUNK]
            scale_x[l] = da[:CHUNK] * jnp.exp(end - la[:CHUNK])
            scale_f[l] = jnp.exp(la[CHUNK:] - end)

    arrived("x", buf_x)
    spread(buf_x, xs)

    for layer in range(LAYERS):

        def named(name, layer=layer):
            return f"{name}{layer}"

        mixed32 = jnp.dot(aperm[layer], xs[...], precision=HI, preferred_element_type=F32)
        mixed = mixed32.astype(BF16)
        mixed32 = mixed.astype(F32)
        for q in range(G // 2):
            lanes = slice(q * PAIR, (q + 1) * PAIR)
            pieces = mix_halves(mixed32[:G, lanes], mixed32[G:, lanes])
            for i in range(2):
                send_a[layer, 2 * q + i] = pieces[i].astype(BF16)
        send("mp", named("a"), lambda peer: send_a.at[layer, peer], buf_a.at[layer])
        buf_a[layer, c] = send_a[layer, c]
        if layer == 1:
            step2(1)
        if layer == 0:
            wait_bytes(rsem, "wb0", flat_wb0)
            weights = wb0[...].reshape(WIDE, PAIR)
        else:
            weights = blk0[:, :, :, :, pl.ds(WIDE, PAIR)].reshape(WIDE, PAIR)
        coef = jnp.dot(mixed, weights, preferred_element_type=F32)
        in_b, out_c = mix_halves(coef[:G], coef[G:])
        for pair in range(USED):
            send_k[layer, pair, :, pl.ds(0, PAIR)] = in_b[pair : pair + 1]
            send_k[layer, pair, :, pl.ds(PAIR, PAIR)] = out_c[pair : pair + 1]
        send_used(named("k"), lambda peer: send_k.at[layer, peer], buf_k.at[layer])

        if layer == 0:
            step1(0)
            step1(1)
        arrived(named("a"), buf_a.at[layer])
        tmp[0] = buf_a[layer].reshape(FRAMES, PAIR).astype(F32)
        for pair in range(USED):
            send_b[layer, pair] = tmp[0, pl.ds(pair, G, stride=G), :].astype(BF16)
        send_used(named("b"), lambda peer: send_b.at[layer, peer], buf_b.at[layer])

        @pl.when(scans)
        def _():
            buf_b[layer, b] = send_b[layer, b]
            buf_k[layer, b] = send_k[layer, b]
            arrived(named("k"), buf_k.at[layer])
            for block in range(G):
                for part in range(2):
                    tmp[1 + part, pl.ds(block, 1)] = buf_k[layer, block, :, pl.ds(part * PAIR, PAIR)]
            for part in range(2):
                send_g[layer, :, pl.ds(part * PAIR, PAIR)] = tmp[1 + part, pl.ds(0, G)].astype(BF16)
            peers(
                "mp",
                lambda peer: copy(
                    named("g"), send_g.at[layer], buf_g.at[layer, c], (b, peer)
                ).start(),
            )
            buf_g[layer, c] = send_g[layer]

        def drain_g(layer=layer):
            @pl.when(scans)
            def _():
                wait_bytes(ssem, f"g{layer}", buf_g.at[layer, pl.ds(0, G - 1)])

        drains.append(drain_g)
        if layer == 0:
            step2(0)
        if layer == 1:
            step2b(1)
        if layer == 0:
            decay_scales()

        @pl.when(scans)
        def _():
            arrived(named("g"), buf_g.at[layer])
            for part in range(2):
                tmp[1 + part] = buf_g[layer, :, :, pl.ds(part * PAIR, PAIR)].reshape(FRAMES, PAIR).astype(F32)
            bp, cp = [
                jnp.concatenate([tmp[1 + part, pl.ds(k, G, stride=G), :] for k in range(G)], axis=0)
                for part in range(2)
            ]
            bp = bp.astype(BF16)
            left = left_half((FRAMES, PAIR))
            causal = lax.broadcasted_iota(jnp.int32, (CHUNK, CHUNK), 1) <= lax.broadcasted_iota(
                jnp.int32, (CHUNK, CHUNK), 0
            )

            def grid(cj, bj, masked):
                g = lax.dot_general(
                    cj, bj, (((1,), (1,)), ((), ())), preferred_element_type=F32
                )
                g = jnp.where(causal, g, 0.0) if masked else g
                first = g.astype(BF16)
                return jnp.concatenate([first, (g - first.astype(F32)).astype(BF16), first], axis=1)

            grids = []
            for j in range(2):
                cj = jnp.where(left if j == 0 else jnp.logical_not(left), cp, 0.0).astype(BF16)
                grids.append(
                    (
                        grid(cj[:CHUNK], bp[:CHUNK], True),
                        grid(cj[CHUNK:], bp[CHUNK:], True),
                        grid(cj[CHUNK:], bp[:CHUNK], False),
                    )
                )
            arrived(named("b"), buf_b.at[layer])
            m = buf_b[layer].reshape(FRAMES, PAIR).astype(F32)
            v = m * scale_w[layer]
            vx = m[:CHUNK] * scale_x[layer]
            values = []
            for p in (v[:CHUNK], v[CHUNK:], vx):
                first = p.astype(BF16)
                rest = (p - first.astype(F32)).astype(BF16)
                values.append(jnp.concatenate([first, first, rest], axis=0))
            y0, y1, yx = [
                jnp.where(
                    left[:CHUNK],
                    jnp.dot(grids[0][i], values[i], preferred_element_type=F32),
                    jnp.dot(grids[1][i], values[i], preferred_element_type=F32),
                )
                for i in range(3)
            ]
            gain = skip[pl.ds(layer, 1), :]
            gain = jnp.concatenate([gain, gain], axis=1)
            low = y0 * scale_e[layer, pl.ds(0, CHUNK)] + gain * m[:CHUNK]
            high = (
                y1 * scale_e[layer, pl.ds(CHUNK, CHUNK)] + yx * scale_f[layer] + gain * m[CHUNK:]
            )
            send_c[layer, pl.ds(0, G // 2)] = low.astype(BF16).reshape(G // 2, G, PAIR)
            send_c[layer, pl.ds(G // 2, G // 2)] = high.astype(BF16).reshape(G // 2, G, PAIR)
            peers(
                "frames",
                lambda peer: copy(
                    named("c"), send_c.at[layer, peer], buf_c.at[layer, b], (peer, c)
                ).start(),
            )
            buf_c[layer, b] = send_c[layer, b]

        def drain_c(layer=layer):
            @pl.when(scans)
            def _():
                wait_bytes(ssem, f"c{layer}", buf_c.at[layer, pl.ds(0, G - 1)])

        drains.append(drain_c)
        if layer == 0:
            step2b(0)
        if layer == 1:
            step3(1)

        @pl.when(scans)
        def _():
            wait_bytes(rsem, named("c"), buf_c.at[layer, pl.ds(0, USED - 1)])

        @pl.when(jnp.logical_not(scans))
        def _():
            wait_bytes(rsem, named("c"), buf_c.at[layer, pl.ds(0, USED)])

        tmp[0] = buf_c[layer].reshape(FRAMES, PAIR).astype(F32)
        for frame in range(G):
            send_d[layer, frame] = tmp[0, pl.ds(frame, G, stride=G), :].astype(BF16)
        send("mp", named("d"), lambda peer: send_d.at[layer, peer], buf_d.at[layer])
        buf_d[layer, c] = send_d[layer, c]

        if layer == 0:
            step3(0)
            step4(0)
        if layer == 1:
            step4(1)
        arrived(named("d"), buf_d.at[layer])
        spread(buf_d.at[layer], res)
        weights = blocks[layer][:, :, :, :, pl.ds(0, WIDE)].reshape(WIDE, WIDE)
        xs[...] += jnp.dot(res[...], weights, preferred_element_type=F32)

    for q in range(G // 2):
        lanes = pl.ds(q * PAIR, PAIR)
        pieces = mix_halves(xs[pl.ds(0, G), lanes], xs[pl.ds(G, G), lanes])
        send_e[2 * q] = pieces[0]
        send_e[2 * q + 1] = pieces[1]
    send("mp", "e", lambda peer: send_e.at[peer], out_ref)
    out_ref[c] = send_e[c]
    for drain in drains:
        drain()
    arrived("e", out_ref)


def shards(motion, adjacency, w_bc, decay, skip, w_out):
    vm = pltpu.VMEM
    part = HALF // 2
    out = pl.pallas_call(
        body,
        out_shape=jax.ShapeDtypeStruct((G, G, PAIR), F32),
        in_specs=[pl.BlockSpec(memory_space=pltpu.HBM)] * 6,
        out_specs=pl.BlockSpec(memory_space=vm),
        scratch_shapes=[
            vm((JOINTS, G, HALF), BF16),
            vm((JOINTS, LAYERS, JOINTS), F32),
            vm((LAYERS, JOINTS, JOINTS), F32),
            vm((LAYERS, G, HALF), F32),
            vm((LAYERS, HALF), F32),
            vm((SIDE, SIDE, 2, part, PAIR), BF16),
            vm((SIDE, SIDE, 2, part, WIDE + PAIR), BF16),
            vm((SIDE, SIDE, 2, part, WIDE), BF16),
            vm((G, PAIR), F32),
            vm((G, G, PAIR), F32),
            vm((LAYERS, FRAMES, PAIR), F32),
            vm((LAYERS, FRAMES, PAIR), F32),
            vm((LAYERS, CHUNK, PAIR), F32),
            vm((LAYERS, CHUNK, PAIR), F32),
            vm((LAYERS, 2 * G, 2 * G), F32),
            vm((G, G, PAIR), BF16),
            vm((G, G, PAIR), BF16),
            vm((LAYERS, G, G, PAIR), BF16),
            vm((LAYERS, G, G, PAIR), BF16),
            vm((LAYERS, USED, 1, 2 * PAIR), F32),
            vm((LAYERS, G, 1, 2 * PAIR), F32),
            vm((LAYERS, G, 2 * PAIR), BF16),
            vm((LAYERS, G, G, 2 * PAIR), BF16),
            vm((LAYERS, USED, G, PAIR), BF16),
            vm((LAYERS, G, G, PAIR), BF16),
            vm((LAYERS, G, G, PAIR), BF16),
            vm((LAYERS, G, G, PAIR), BF16),
            vm((LAYERS, G, G, PAIR), BF16),
            vm((LAYERS, G, G, PAIR), BF16),
            vm((G, G, PAIR), F32),
            vm((G, G, PAIR), F32),
            vm((3, FRAMES, PAIR), F32),
            vm((2 * G, WIDE), F32),
            vm((2 * G, WIDE), BF16),
            pltpu.SemaphoreType.DMA((8,)),
            pltpu.SemaphoreType.DMA((24,)),
            pltpu.SemaphoreType.DMA((24,)),
        ],
        compiler_params=pltpu.CompilerParams(
            collective_id=0, has_side_effects=True, vmem_limit_bytes=56 * 2**20
        ),
    )(
        motion.transpose(1, 0, 2),
        adjacency.transpose(1, 0, 2),
        w_bc.reshape(LAYERS, 2, part, PAIR),
        decay,
        skip,
        w_out.reshape(LAYERS, 2, part, WIDE),
    )
    return out.reshape(G, 2 * G, HALF)[:, :JOINTS]


def solution(mesh):
    return jax.shard_map(
        shards,
        mesh=mesh,
        in_specs=(
            P("frames", None, "mp"),
            P(),
            P(None, "mp", None),
            P(None, "frames", "mp"),
            P(None, "mp"),
            P(None, "mp", None),
        ),
        out_specs=P("frames", None, "mp"),
        check_vma=False,
    )
```
